32 devices in a mesh: groups: 2 (over y), ctx: 4 (over x, core), dp: 4 (over z).
Axes of the slice: x: 2, y: 2, z: 4, core: 2. Of those that a mesh axis runs over, the one named last changes fastest.
Arguments:
- tokens: bfloat16 [8, 512, 1024], P(('groups', 'dp'), 'ctx'), parts along dimension 0, may hold values from -24 to 24
- global_blocks: int32 [8, 2], P(('groups', 'dp')), parts along dimension 0, may hold values from 0 to 7, as said below
- w_query: bfloat16 [1024, 1024], P('dp'), may hold values from -0.125 to 0.125
- w_key: bfloat16 [1024, 1024], P('dp'), may hold values from -0.125 to 0.125
- w_value: bfloat16 [1024, 1024], P('dp'), may hold values from -0.1875 to 0.1875
- d_context: bfloat16 [8, 512, 1024], P(('groups', 'dp'), 'ctx'), parts along dimension 0, may hold values from -6 to 6
Outputs:
- context: bfloat16 [8, 512, 1024], P(('groups', 'dp'), 'ctx'), parts along dimension 0
- grad_tokens: bfloat16 [8, 512, 1024], P(('groups', 'dp'), 'ctx'), parts along dimension 0
- grad_w_query: float32 [2048, 1024], P(('groups', 'dp'), 'ctx'), parts along dimension 0
- grad_w_key: float32 [2048, 1024], P(('groups', 'dp'), 'ctx'), parts along dimension 0
- grad_w_value: float32 [2048, 1024], P(('groups', 'dp'), 'ctx'), parts along dimension 0
The draws below stay inside these ranges and needn't reach their ends.
There are 2 independent parts, one for each index of `groups`. The reference program is written for one: setup_inputs(seed, part) draws one part's arguments, and reference() takes and returns one part's arrays. A program takes and returns all parts, laid end to end along the dimension named above; an argument that names none is the same for every part. Nothing has to cross between parts.
Inputs may be any that keep to these rules, and one draw needn't show every extreme that they name: `global_blocks`: each sequence names two different blocks.
All inputs are finite; a program needn't handle non-finite values.
Results may differ from the reference program's by a relative error of at most 0.015.
The reference program's roundings to bfloat16 on the way count: a program that leaves them out, or rounds other values in their place, can miss the bound.
Values may be sent and summed in bfloat16 or wider, within the bound.
No kernel may reach another device: no remote copies, remote signals or barrier semaphores. Data moves between devices by JAX's collectives and lax.ppermute only.
A program may use at most 128 MiB of HBM per device.

```python
import math
import jax
import jax.numpy as jnp
from jax import lax

D = 1024
HEADS = 16
BLK = 64
SEQ_LEN = 512
SEQS = 4


def draw_tokens(key, part):
    base = jnp.clip(jax.random.normal(jax.random.fold_in(key, 1), (SEQS, SEQ_LEN, D), jnp.float32), -4.0, 4.0)
    return base.astype(jnp.bfloat16)


def weight_pair(key):
    first = jax.random.normal(jax.random.fold_in(key, 21), (D, D), jnp.float32)
    second = jax.random.normal(jax.random.fold_in(key, 22), (D, D), jnp.float32)
    first = jnp.clip(first, -4.0, 4.0) / math.sqrt(D)
    second = jnp.clip(second, -4.0, 4.0) / math.sqrt(D)
    return (first, second)


def draw_w_query(key, part):
    return weight_pair(key)[0].astype(jnp.bfloat16)


def draw_w_key(key, part):
    return weight_pair(key)[1].astype(jnp.bfloat16)


def draw_global_blocks(key, part):
    block_total = SEQ_LEN // BLK
    first = jax.random.randint(jax.random.fold_in(key, 31), (SEQS,), 0, block_total)
    stride = jax.random.randint(jax.random.fold_in(key, 32), (SEQS,), 1, block_total)
    second = (first + stride) % block_total
    return jnp.stack([first, second], axis=1).astype(jnp.int32)


def with_spikes(values, rng, source, target, parts, factor):
    def block_of(position):
        return (jnp.arange(values.shape[position]) // (values.shape[position] // parts)).reshape((-1,) + (1,) * (values.ndim - 1 - position))

    first = jax.random.permutation(rng, parts)[block_of(target)]
    other_side = (block_of(target) + parts // 2) % parts
    return jnp.where((block_of(source) == first) | (block_of(source) == other_side), factor * values, values)


def block_levels(own_key, shape, cuts, low, largest):
    def one(axis_at, parts):
        draws = jax.random.uniform(jax.random.fold_in(jax.random.fold_in(own_key, 6), axis_at), (parts,), jnp.float32, low / len(cuts), largest / len(cuts))
        return jnp.repeat(jnp.exp(draws), shape[axis_at] // parts).reshape((-1,) + (1,) * (len(shape) - axis_at - 1))

    factor_of = one(*cuts[0])
    for cut in cuts[1:]:
        factor_of = factor_of * one(*cut)
    return factor_of


def normal_values(rng, shape, width, reach, cuts=(), kind=jnp.bfloat16):
    entries = width * jax.random.normal(rng, shape, jnp.float32)
    if cuts:
        entries = entries * block_levels(rng, shape, cuts, -0.22, 0.18)
    return jnp.clip(entries, -reach, reach).astype(kind)


def noise_with(key, extent, deviation, reach, split, heavy, held_as=jnp.bfloat16):
    drawn = deviation * jax.random.normal(key, extent, jnp.float32)
    if split:
        drawn = drawn * block_levels(key, extent, split, -0.22, 0.18)
    return jnp.clip(with_spikes(drawn, jax.random.fold_in(key, 3), *heavy), -reach, reach).astype(held_as)


def setup_inputs(seed: int = 0, part: int = 0) -> dict:
    arg_keys = jax.random.split(jax.random.key(seed), 7)
    own_keys = jax.random.split(jax.random.fold_in(arg_keys[6], part), 7)
    return {
        "tokens": draw_tokens(jax.random.fold_in(jax.random.fold_in(arg_keys[6], part), 71), part),
        "global_blocks": draw_global_blocks(jax.random.fold_in(jax.random.fold_in(arg_keys[6], part), 71), part),
        "w_query": draw_w_query(jax.random.fold_in(arg_keys[6], 71), part),
        "w_key": draw_w_key(jax.random.fold_in(arg_keys[6], 71), part),
        "w_value": normal_values(arg_keys[4], (D, D), D ** -0.5, 0.1875, ((0, 4),)),
        "d_context": noise_with(own_keys[5], (SEQS, SEQ_LEN, D), 1.0, 6.0, ((0, 4), (1, 4)), (1, 2, 4, 2.0)),
    }


NEG = -1e+30

def rounded(values):
    return lax.optimization_barrier(values.astype(jnp.bfloat16)).astype(jnp.float32)

def block_masks(first_block, block_count, all_blocks, chosen_blocks):
    blocks = first_block + jnp.arange(block_count, dtype=jnp.int32)
    near = blocks[:, None] - 1 + jnp.arange(3, dtype=jnp.int32)[None, :]
    near_ok = (near >= 0) & (near < all_blocks)
    far_ok = jnp.abs(chosen_blocks[None, :] - blocks[:, None]) > 1
    keep = jnp.repeat(jnp.concatenate([near_ok, far_ok], axis=1), BLK, axis=1)
    chosen = (blocks == chosen_blocks[0]) | (blocks == chosen_blocks[1])
    return (keep, chosen)

def window_rows(blocked, extra, block_count, model_width, heads):
    padded = jnp.pad(blocked, ((1, 1), (0, 0), (0, 0)))
    near = jnp.concatenate([padded[:-2], padded[1:-1], padded[2:]], axis=1)
    far = jnp.broadcast_to(extra[None], (block_count, 2 * BLK, model_width))
    return jnp.concatenate([near, far], axis=1).reshape(block_count, 5 * BLK, heads, model_width // heads)

def reference(tokens, global_blocks, w_query, w_key, w_value, d_context):
    model_width = D
    hdim = model_width // HEADS
    block_count = SEQ_LEN // BLK
    score_scale = 1.0 / math.sqrt(hdim)
    weight_set = (w_query, w_key, w_value)

    def one_sequence(carry, item):
        inputs, chosen_blocks, upstream = item
        queries, key_rows, value_rows = [jnp.dot(inputs, weight, preferred_element_type=jnp.float32).astype(jnp.bfloat16) for weight in weight_set]
        keep, chosen = block_masks(0, block_count, block_count, chosen_blocks)
        q_blocks = queries.reshape(block_count, BLK, model_width)
        k_blocks = key_rows.reshape(block_count, BLK, model_width)
        v_blocks = value_rows.reshape(block_count, BLK, model_width)
        up_blocks = upstream.reshape(block_count, BLK, model_width)
        global_query = q_blocks[chosen_blocks].reshape(2 * BLK, HEADS, hdim).astype(jnp.float32)
        global_key = k_blocks[chosen_blocks].reshape(2 * BLK, model_width)
        global_value = v_blocks[chosen_blocks].reshape(2 * BLK, model_width)
        global_up = up_blocks[chosen_blocks].reshape(2 * BLK, HEADS, hdim).astype(jnp.float32)
        window_key = window_rows(k_blocks, global_key, block_count, model_width, HEADS).astype(jnp.float32)
        window_value = window_rows(v_blocks, global_value, block_count, model_width, HEADS).astype(jnp.float32)
        query_heads = queries.reshape(block_count, BLK, HEADS, hdim).astype(jnp.float32)
        scores = jnp.einsum('nqhe,nkhe->nhqk', query_heads, window_key) * score_scale
        scores = jnp.where(keep[:, None, None, :], scores, NEG)
        row_max = lax.optimization_barrier(jnp.max(scores, axis=-1, keepdims=True))
        raw = jnp.exp(scores - row_max)
        row_sum = lax.optimization_barrier(jnp.sum(raw, axis=-1, keepdims=True))
        window_out = jnp.einsum('nhqk,nkhe->nqhe', rounded(raw), window_value) / jnp.transpose(row_sum, (0, 2, 1, 3))
        key_heads = key_rows.reshape(SEQ_LEN, HEADS, hdim).astype(jnp.float32)
        value_heads = value_rows.reshape(SEQ_LEN, HEADS, hdim).astype(jnp.float32)
        global_scores = jnp.einsum('qhe,khe->hqk', global_query, key_heads) * score_scale
        global_max = lax.optimization_barrier(jnp.max(global_scores, axis=-1, keepdims=True))
        global_raw = jnp.exp(global_scores - global_max)
        global_sum = lax.optimization_barrier(jnp.sum(global_raw, axis=-1, keepdims=True))
        global_out = jnp.einsum('hqk,khe->qhe', rounded(global_raw), value_heads) / jnp.transpose(global_sum, (1, 0, 2))
        merged = window_out.reshape(block_count, BLK, model_width)
        merged = merged.at[chosen_blocks].set(global_out.reshape(2, BLK, model_width))
        context = merged.reshape(SEQ_LEN, model_width).astype(jnp.bfloat16)
        up_heads = upstream.reshape(block_count, BLK, HEADS, hdim)
        window_up = jnp.where(chosen[:, None, None, None], jnp.zeros_like(up_heads), up_heads).astype(jnp.float32)
        probs = raw / row_sum
        grad_probs = jnp.einsum('nqhe,nkhe->nhqk', window_up, window_value)
        delta = jnp.transpose(lax.optimization_barrier(jnp.sum(window_up * window_out, axis=-1)), (0, 2, 1))
        grad_low = rounded(probs * (grad_probs - delta[..., None]))
        grad_query = score_scale * jnp.einsum('nhqk,nkhe->nqhe', grad_low, window_key)
        grad_keys = score_scale * jnp.einsum('nhqk,nqhe->nkhe', grad_low, query_heads)
        grad_values = jnp.einsum('nhqk,nqhe->nkhe', rounded(probs), window_up)
        stacked = jnp.stack([grad_keys, grad_values]).reshape(2, block_count, 5 * BLK, model_width)
        spread = jnp.pad(stacked[:, :, :BLK], ((0, 0), (0, 2), (0, 0), (0, 0)))
        spread = spread + jnp.pad(stacked[:, :, BLK:2 * BLK], ((0, 0), (1, 1), (0, 0), (0, 0)))
        spread = spread + jnp.pad(stacked[:, :, 2 * BLK:3 * BLK], ((0, 0), (2, 0), (0, 0), (0, 0)))
        inner = spread[:, 1:-1]
        far_grad = lax.optimization_barrier(jnp.sum(stacked[:, :, 3 * BLK:], axis=1))
        global_probs = global_raw / global_sum
        global_grad_probs = jnp.einsum('qhe,khe->hqk', global_up, value_heads)
        global_delta = jnp.transpose(lax.optimization_barrier(jnp.sum(global_up * global_out, axis=-1)))
        global_low = rounded(global_probs * (global_grad_probs - global_delta[..., None]))
        global_query_grad = score_scale * jnp.einsum('hqk,khe->qhe', global_low, key_heads)
        key_from_global = score_scale * jnp.einsum('hqk,qhe->khe', global_low, global_query)
        value_from_global = jnp.einsum('hqk,qhe->khe', rounded(global_probs), global_up)
        grad_q = grad_query.reshape(block_count, BLK, model_width)
        grad_q = grad_q.at[chosen_blocks].add(global_query_grad.reshape(2, BLK, model_width))
        grad_k = inner[0] + key_from_global.reshape(block_count, BLK, model_width)
        grad_k = grad_k.at[chosen_blocks].add(far_grad[0].reshape(2, BLK, model_width))
        grad_v = inner[1] + value_from_global.reshape(block_count, BLK, model_width)
        grad_v = grad_v.at[chosen_blocks].add(far_grad[1].reshape(2, BLK, model_width))
        grads_low = [grad.reshape(SEQ_LEN, model_width).astype(jnp.bfloat16) for grad in (grad_q, grad_k, grad_v)]
        grad_in = jnp.zeros((SEQ_LEN, model_width), jnp.float32)
        for grad, weight in zip(grads_low, weight_set):
            grad_in = grad_in + jnp.dot(grad, weight.T, preferred_element_type=jnp.float32)
        terms = jnp.stack([jnp.dot(inputs.T, grad, preferred_element_type=jnp.float32) for grad in grads_low])
        return (carry + terms, (context, grad_in.astype(jnp.bfloat16)))
    start = jnp.zeros((3, model_width, model_width), jnp.float32)
    totals, (context, grad_tokens) = lax.scan(one_sequence, start, (tokens, global_blocks, d_context))
    return (context, grad_tokens, totals[0], totals[1], totals[2])
```

```python
import math

import jax
import jax.numpy as jnp
from jax import lax
from jax.experimental import pallas as pl
from jax.experimental.pallas import tpu as pltpu
from jax.sharding import PartitionSpec as P

HEADS = 16
BLK = 64
NEG = -1e30
SPLIT = 1

NT = (((1,), (1,)), ((), ()))
TN = (((0,), (0,)), ((), ()))
F32 = jnp.float32
BF16 = jnp.bfloat16


def xor_permute(value, axis, bit):
    count = lax.axis_size(axis)
    return lax.ppermute(value, axis, [(i, i ^ bit) for i in range(count)])


def attention_kernel(
    where_ref, chosen_ref, *refs, seqs, chunks, rows, heads, hdim, parts, scale
):
    pieces = seqs * chunks
    token_refs = refs[:pieces]
    up_refs = refs[pieces : 2 * pieces]
    weight_refs = refs[2 * pieces : 2 * pieces + parts]
    context_ref, grad_in_ref, grad_w_ref = refs[2 * pieces + parts : 2 * pieces + parts + 3]
    all_tokens, weight, q_s, k_s, v_s, up_s, dk_s, dv_s, grads = refs[2 * pieces + parts + 3 :]
    length = chunks * rows
    width = heads * hdim
    model = all_tokens.shape[1]
    part_rows = model // parts
    position = where_ref[0]
    line = where_ref[1]

    for j in range(parts):
        start = pl.multiple_of((line ^ j) * part_rows, part_rows)
        weight[pl.ds(start, part_rows), :] = weight_refs[j][...]
    for b in range(pieces):
        all_tokens[b * rows : (b + 1) * rows, :] = token_refs[b][...]
        for h in range(heads):
            up_s[h, b * rows : (b + 1) * rows, :] = up_refs[b][:, h * hdim : (h + 1) * hdim]

    tile = min(256, length)

    @pl.loop(0, seqs * length // tile)
    def _(t):
        at = pl.ds(pl.multiple_of(t * tile, tile), tile)
        out = jnp.dot(all_tokens[at, :], weight[...], preferred_element_type=F32)
        for h in range(heads):
            lo = h * hdim
            q_s[h, at, :] = (out[:, lo : lo + hdim].astype(BF16) * scale).astype(BF16)
            k_s[h, at, :] = out[:, width + lo : width + lo + hdim].astype(BF16)
            v_s[h, at, :] = out[:, 2 * width + lo : 2 * width + lo + hdim].astype(BF16)

    dk_s[...] = jnp.zeros_like(dk_s)
    dv_s[...] = jnp.zeros_like(dv_s)
    blocks_per_chunk = rows // BLK

    @pl.loop(0, pieces)
    def _(b):
        i = b // chunks
        j = b - i * chunks
        at = pl.ds(pl.multiple_of(b * rows, rows), rows)
        keys_at = pl.ds(pl.multiple_of(i * length, length), length)
        first = chosen_ref[2 * i]
        second = chosen_ref[2 * i + 1]
        key_pos = lax.broadcasted_iota(jnp.int32, (length, rows), 0)
        query_pos = lax.broadcasted_iota(jnp.int32, (length, rows), 1)
        key_block = (lax.shift_right_logical(key_pos, int(math.log2(rows))) ^ position) * (
            blocks_per_chunk
        ) + lax.shift_right_logical(key_pos & (rows - 1), int(math.log2(BLK)))
        query_block = (position ^ j) * blocks_per_chunk + lax.shift_right_logical(
            query_pos, int(math.log2(BLK))
        )
        keep = (
            (jnp.abs(key_block - query_block) <= 1)
            | (key_block == first)
            | (key_block == second)
            | (query_block == first)
            | (query_block == second)
        )
        for h in range(heads):
            q = q_s[h, at, :]
            k = k_s[h, keys_at, :]
            v = v_s[h, keys_at, :]
            up = up_s[h, at, :]
            scores = lax.dot_general(k, q, NT, preferred_element_type=F32)
            scores = jnp.where(keep, scores, NEG)
            top = jnp.max(scores, axis=0, keepdims=True)
            raw = jnp.exp(scores - top)
            inverse = 1.0 / jnp.sum(raw, axis=0, keepdims=True)
            out_t = lax.dot_general(v, raw.astype(BF16), TN, preferred_element_type=F32) * inverse
            probs = raw * inverse
            grad_probs = lax.dot_general(v, up, NT, preferred_element_type=F32)
            delta = jnp.sum(jnp.transpose(up.astype(F32)) * out_t, axis=0, keepdims=True)
            low = (probs * (grad_probs - delta)).astype(BF16)
            grad_q = lax.dot_general(k, low, TN, preferred_element_type=F32) * scale
            dk_s[h, keys_at, :] += jnp.dot(low, q, preferred_element_type=F32)
            dv_s[h, keys_at, :] += jnp.dot(probs.astype(BF16), up, preferred_element_type=F32)
            lo = h * hdim
            context_ref[at, lo : lo + hdim] = jnp.transpose(out_t).astype(BF16)
            grads[at, lo : lo + hdim] = jnp.transpose(grad_q).astype(BF16)

    for h in range(heads):
        lo = h * hdim
        grads[:, width + lo : width + lo + hdim] = dk_s[h].astype(BF16)
        grads[:, 2 * width + lo : 2 * width + lo + hdim] = dv_s[h].astype(BF16)

    @pl.loop(0, seqs * length // tile)
    def _(t):
        at = pl.ds(pl.multiple_of(t * tile, tile), tile)
        grad_in_ref[at, :] = lax.dot_general(
            grads[at, :], weight[...], NT, preferred_element_type=F32
        ).astype(BF16)

    @pl.loop(0, parts)
    def _(j):
        cols = pl.ds(pl.multiple_of((line ^ j) * part_rows, part_rows), part_rows)
        grad_w_ref[j] = lax.dot_general(
            all_tokens[:, cols], grads[...], TN, preferred_element_type=F32
        ).astype(BF16)


def per_device(tokens, global_blocks, w_query, w_key, w_value, d_context):
    own_tokens = tokens[0]
    upstream = d_context[0]
    rows, model = own_tokens.shape
    hdim = model // HEADS
    chunks = lax.axis_size("ctx")
    parts = lax.axis_size("dp")
    seqs = SPLIT if HEADS % (SPLIT * chunks) == 0 and parts % SPLIT == 0 else 1
    groups = chunks * seqs
    width = model // groups
    heads = width // hdim
    position = lax.axis_index("ctx")
    line = lax.axis_index("dp")
    side = line % seqs

    hops = [("dp", 1, chunks)] if seqs == 2 else []
    bit = chunks // 2
    while bit:
        hops.append(("ctx", bit, bit))
        bit //= 2

    def slice_of(value, offset):
        which = (position ^ (offset % chunks)) * seqs + (side ^ (offset // chunks))
        return lax.dynamic_slice_in_dim(value, which * width, width, 1)

    sends = []
    for i in range(seqs):
        sends.append(
            jnp.concatenate(
                [slice_of(w, i * chunks) for w in (w_query, w_key, w_value)], axis=1
            )
        )
    weights = [sends[0]]
    for j in range(1, parts):
        weights.append(xor_permute(sends[j % seqs], "dp", j))

    token_pieces = {0: own_tokens}
    up_pieces = {0: jnp.concatenate([slice_of(upstream, o) for o in range(groups)], axis=1)}
    chosen = [global_blocks[0]]
    for axis, bit, offset in hops:
        for key in list(token_pieces):
            token_pieces[key + offset] = xor_permute(token_pieces[key], axis, bit)
        if axis == "dp":
            chosen.append(xor_permute(global_blocks, axis, bit)[0])
        for key in list(up_pieces):
            held = up_pieces[key]
            half = held.shape[1] // 2
            up_pieces[key + offset] = xor_permute(held[:, half:], axis, bit)
            up_pieces[key] = held[:, :half]

    length = chunks * rows
    total = seqs * length
    context, grad_in, grad_w = pl.pallas_call(
        lambda *refs: attention_kernel(
            *refs,
            seqs=seqs,
            chunks=chunks,
            rows=rows,
            heads=heads,
            hdim=hdim,
            parts=parts,
            scale=1.0 / math.sqrt(hdim),
        ),
        out_shape=(
            jax.ShapeDtypeStruct((total, width), BF16),
            jax.ShapeDtypeStruct((total, model), BF16),
            jax.ShapeDtypeStruct((parts, model // parts, 3 * width), BF16),
        ),
        in_specs=[pl.BlockSpec(memory_space=pltpu.SMEM)] * 2
        + [pl.BlockSpec(memory_space=pltpu.VMEM)] * (2 * groups + parts),
        out_specs=(pl.BlockSpec(memory_space=pltpu.VMEM),) * 3,
        scratch_shapes=[
            pltpu.VMEM((total, model), BF16),
            pltpu.VMEM((model, 3 * width), BF16),
            pltpu.VMEM((heads, total, hdim), BF16),
            pltpu.VMEM((heads, total, hdim), BF16),
            pltpu.VMEM((heads, total, hdim), BF16),
            pltpu.VMEM((heads, total, hdim), BF16),
            pltpu.VMEM((heads, total, hdim), F32),
            pltpu.VMEM((heads, total, hdim), F32),
            pltpu.VMEM((total, 3 * width), BF16),
        ],
        compiler_params=pltpu.CompilerParams(vmem_limit_bytes=48 * 1024 * 1024),
        name="attention",
    )(
        jnp.stack([position, line]).astype(jnp.int32),
        jnp.concatenate(chosen),
        *[token_pieces[o] for o in range(groups)],
        *[up_pieces[o] for o in range(groups)],
        *weights,
    )

    moved = [grad_w[0]] + [xor_permute(grad_w[j], "dp", j) for j in range(1, parts)]
    sums = []
    for i in range(seqs):
        acc = moved[i].astype(F32)
        for j in range(i + seqs, parts, seqs):
            acc = acc + moved[j].astype(F32)
        sums.append(acc.reshape(-1, 3, width))
    if seqs == 2:
        low = jnp.where(side == 0, sums[0], sums[1])
        high = jnp.where(side == 0, sums[1], sums[0])
        final = jnp.concatenate([low, high], axis=2)
    else:
        final = sums[0]

    grad_in = grad_in.reshape(groups, rows, model)
    for axis, bit, _ in reversed(hops):
        view = grad_in.reshape(-1, 2, rows, model)
        got = xor_permute(view[:, 1], axis, bit)
        grad_in = (view[:, 0].astype(F32) + got.astype(F32)).astype(BF16)
    grad_tokens = grad_in

    context = context.reshape(groups, rows, width)
    back = [context[0]]
    for o in range(1, groups):
        value = context[o]
        if o % chunks:
            value = xor_permute(value, "ctx", o % chunks)
        if o // chunks:
            value = xor_permute(value, "dp", o // chunks)
        back.append(value)
    stacked = jnp.stack(back)
    index = jnp.arange(groups, dtype=jnp.int32)
    home = ((index // seqs) ^ position) + ((index % seqs) ^ side) * chunks
    full = jnp.take(stacked, home, axis=0)
    full = jnp.transpose(full, (1, 0, 2)).reshape(rows, model)
    return (full[None], grad_tokens, final[:, 0], final[:, 1], final[:, 2])


def solution(mesh):
    return jax.shard_map(
        per_device,
        mesh=mesh,
        in_specs=(
            P(("groups", "dp"), "ctx", None),
            P(("groups", "dp"), None),
            P("dp", None),
            P("dp", None),
            P("dp", None),
            P(("groups", "dp"), "ctx", None),
        ),
        out_specs=(
            P(("groups", "dp"), "ctx", None),
            P(("groups", "dp"), "ctx", None),
            P(("groups", "dp"), "ctx"),
            P(("groups", "dp"), "ctx"),
            P(("groups", "dp"), "ctx"),
        ),
        check_vma=False,
    )
```

```python
import math

import jax
import jax.numpy as jnp
from jax import lax
from jax.experimental import pallas as pl
from jax.experimental.pallas import tpu as pltpu
from jax.sharding import PartitionSpec as P

HEADS = 16
BLK = 64
NEG = -1e30
SPLIT = 2

NT = (((1,), (1,)), ((), ()))
TN = (((0,), (0,)), ((), ()))
F32 = jnp.float32
BF16 = jnp.bfloat16


def xor_permute(value, axis, bit):
    count = lax.axis_size(axis)
    return lax.ppermute(value, axis, [(i, i ^ bit) for i in range(count)])


def attention_kernel(
    where_ref, chosen_ref, *refs, seqs, chunks, rows, heads, hdim, parts, scale, up_starts
):
    pieces = seqs * chunks
    half = pieces // 2
    token_refs = refs[:pieces]
    up_refs = refs[pieces : 2 * pieces]
    weight_refs = refs[2 * pieces : 2 * pieces + parts]
    outs = refs[2 * pieces + parts :]
    grad_w_refs = outs[:parts]
    keep_ref, send_ref = outs[parts : parts + 2]
    all_tokens, weight, up_all, q_s, k_s, v_s, up_s, dk_s, dv_s, grads, context_s, sems = outs[
        parts + 2 :
    ]
    length = chunks * rows
    width = heads * hdim
    model = all_tokens.shape[1]
    part_rows = model // parts
    position = where_ref[0]
    line = where_ref[1]

    copies = []
    for j in range(parts):
        start = pl.multiple_of((line ^ j) * part_rows, part_rows)
        copies.append((weight_refs[j], weight.at[pl.ds(start, part_rows), :]))
    for b in range(pieces):
        copies.append((token_refs[b].at[:, :model], all_tokens.at[pl.ds(b * rows, rows), :]))
    for b in range(pieces):
        source = up_refs[b]
        start = up_starts[b]
        copies.append((source.at[:, start : start + width], up_all.at[pl.ds(b * rows, rows), :]))
    copies = [
        pltpu.make_async_copy(source, target, sems.at[index])
        for index, (source, target) in enumerate(copies)
    ]
    for copy in copies:
        copy.start()
    for copy in copies:
        copy.wait()
    for h in range(heads):
        up_s[h] = up_all[:, h * hdim : (h + 1) * hdim]

    tile = min(256, length)

    @pl.loop(0, seqs * length // tile)
    def _(t):
        at = pl.ds(pl.multiple_of(t * tile, tile), tile)
        out = jnp.dot(all_tokens[at, :], weight[...], preferred_element_type=F32)
        for h in range(heads):
            lo = h * hdim
            q_s[h, at, :] = (out[:, lo : lo + hdim].astype(BF16) * scale).astype(BF16)
            k_s[h, at, :] = out[:, width + lo : width + lo + hdim].astype(BF16)
            v_s[h, at, :] = out[:, 2 * width + lo : 2 * width + lo + hdim].astype(BF16)

    dk_s[...] = jnp.zeros_like(dk_s)
    dv_s[...] = jnp.zeros_like(dv_s)
    blocks_per_chunk = rows // BLK

    @pl.loop(0, pieces)
    def _(b):
        i = b // chunks
        j = b - i * chunks
        at = pl.ds(pl.multiple_of(b * rows, rows), rows)
        keys_at = pl.ds(pl.multiple_of(i * length, length), length)
        first = chosen_ref[2 * i]
        second = chosen_ref[2 * i + 1]
        key_pos = lax.broadcasted_iota(jnp.int32, (length, rows), 0)
        query_pos = lax.broadcasted_iota(jnp.int32, (length, rows), 1)
        key_block = (lax.shift_right_logical(key_pos, int(math.log2(rows))) ^ position) * (
            blocks_per_chunk
        ) + lax.shift_right_logical(key_pos & (rows - 1), int(math.log2(BLK)))
        query_block = (position ^ j) * blocks_per_chunk + lax.shift_right_logical(
            query_pos, int(math.log2(BLK))
        )
        keep = (
            (jnp.abs(key_block - query_block) <= 1)
            | (key_block == first)
            | (key_block == second)
            | (query_block == first)
            | (query_block == second)
        )
        for h in range(heads):
            q = q_s[h, at, :]
            k = k_s[h, keys_at, :]
            v = v_s[h, keys_at, :]
            up = up_s[h, at, :]
            scores = lax.dot_general(k, q, NT, preferred_element_type=F32)
            scores = jnp.where(keep, scores, NEG)
            top = jnp.max(scores, axis=0, keepdims=True)
            raw = jnp.exp(scores - top)
            inverse = 1.0 / jnp.sum(raw, axis=0, keepdims=True)
            out_t = lax.dot_general(v, raw.astype(BF16), TN, preferred_element_type=F32) * inverse
            probs = raw * inverse
            grad_probs = lax.dot_general(v, up, NT, preferred_element_type=F32)
            delta = jnp.sum(jnp.transpose(up.astype(F32)) * out_t, axis=0, keepdims=True)
            low = (probs * (grad_probs - delta)).astype(BF16)
            grad_q = lax.dot_general(k, low, TN, preferred_element_type=F32) * scale
            dk_s[h, keys_at, :] += jnp.dot(low, q, preferred_element_type=F32)
            dv_s[h, keys_at, :] += jnp.dot(probs.astype(BF16), up, preferred_element_type=F32)
            lo = h * hdim
            context_s[at, lo : lo + hdim] = jnp.transpose(out_t).astype(BF16)
            grads[at, lo : lo + hdim] = jnp.transpose(grad_q).astype(BF16)

    for h in range(heads):
        lo = h * hdim
        grads[:, width + lo : width + lo + hdim] = dk_s[h].astype(BF16)
        grads[:, 2 * width + lo : 2 * width + lo + hdim] = dv_s[h].astype(BF16)

    for j in range(parts):
        cols = pl.ds(pl.multiple_of((line ^ j) * part_rows, part_rows), part_rows)
        grad_w_refs[j][...] = lax.dot_general(
            all_tokens[:, cols], grads[...], TN, preferred_element_type=F32
        ).astype(BF16)

    @pl.loop(0, half)
    def _(t):
        at = pl.ds(pl.multiple_of(t * 2 * rows, 2 * rows), 2 * rows)
        out = lax.dot_general(grads[at, :], weight[...], NT, preferred_element_type=F32)
        keep_ref[t, :, :model] = out[:rows].astype(BF16)
        send_ref[t, :, :model] = out[rows:].astype(BF16)
        keep_ref[t, :, model:] = context_s[pl.ds(pl.multiple_of(t * 2 * rows, rows), rows), :]
        send_ref[t, :, model:] = context_s[
            pl.ds(pl.multiple_of(t * 2 * rows + rows, rows), rows), :
        ]


def add_and_join(mine, theirs, model):
    total = (mine[:, :model].astype(F32) + theirs[:, :model].astype(F32)).astype(BF16)
    return [total, mine[:, model:], theirs[:, model:]]


def combine_kernel(*refs, model):
    count = len(refs) - 2
    keep_ref, got_ref = refs[:2]
    for t in range(count):
        out_ref = refs[2 + t]
        lo = 0
        for value in add_and_join(keep_ref[t], got_ref[t], model):
            out_ref[:, lo : lo + value.shape[1]] = value
            lo += value.shape[1]


def join_kernel(mine_ref, theirs_ref, out_ref, *, model):
    lo = 0
    for value in add_and_join(mine_ref[...], theirs_ref[...], model):
        out_ref[:, lo : lo + value.shape[1]] = value
        lo += value.shape[1]


def final_kernel(where_ref, mine_ref, theirs_ref, grad_ref, context_ref, *, model, seqs, chunks):
    total, mine, theirs = add_and_join(mine_ref[...], theirs_ref[...], model)
    grad_ref[...] = total
    groups = seqs * chunks
    width = model // groups
    values = [mine[:, k * width : (k + 1) * width] for k in range(groups // 2)]
    values += [theirs[:, k * width : (k + 1) * width] for k in range(groups // 2)]
    own = where_ref[0] + where_ref[2] * chunks
    bit = 1
    while bit < groups:
        flip = (own & bit) != 0
        values = [jnp.where(flip, values[o ^ bit], values[o]) for o in range(groups)]
        bit *= 2
    for o in range(groups):
        lo = ((o % chunks) * seqs + o // chunks) * width
        context_ref[:, lo : lo + width] = values[o]


def sum_kernel(where_ref, *refs, parts, seqs, width):
    outs = refs[parts:]
    for m in range(3):
        sums = []
        for i in range(seqs):
            acc = refs[i][:, m * width : (m + 1) * width].astype(F32)
            for j in range(i + seqs, parts, seqs):
                acc = acc + refs[j][:, m * width : (m + 1) * width].astype(F32)
            sums.append(acc)
        if seqs == 1:
            outs[m][...] = sums[0]
        else:
            flip = where_ref[2] != 0
            outs[m][:, :width] = jnp.where(flip, sums[1], sums[0])
            outs[m][:, width:] = jnp.where(flip, sums[0], sums[1])


def per_device(tokens, global_blocks, w_query, w_key, w_value, d_context):
    own_tokens = tokens[0]
    upstream = d_context[0]
    rows, model = own_tokens.shape
    hdim = model // HEADS
    chunks = lax.axis_size("ctx")
    parts = lax.axis_size("dp")
    seqs = SPLIT if HEADS % (SPLIT * chunks) == 0 and parts % SPLIT == 0 else 1
    groups = chunks * seqs
    width = model // groups
    heads = width // hdim
    position = lax.axis_index("ctx")
    line = lax.axis_index("dp")
    side = line % seqs

    where = jnp.stack([position, line, side]).astype(jnp.int32)
    hops = [("dp", 1, chunks)] if seqs == 2 else []
    bit = chunks // 2
    while bit:
        hops.append(("ctx", bit, bit))
        bit //= 2

    def slice_of(value, offset):
        which = (position ^ (offset % chunks)) * seqs + (side ^ (offset // chunks))
        return lax.dynamic_slice_in_dim(value, which * width, width, 1)

    sends = []
    for i in range(seqs):
        sends.append(
            jnp.concatenate(
                [slice_of(w, i * chunks) for w in (w_query, w_key, w_value)], axis=1
            )
        )
    weights = [sends[0]]
    for j in range(1, parts):
        weights.append(xor_permute(sends[j % seqs], "dp", j))

    ups = [slice_of(upstream, o) for o in range(groups)]
    pieces = {0: None}
    chosen = [global_blocks[0]]
    left = groups
    for axis, bit, offset in hops:
        left //= 2
        for key in list(pieces):
            held = pieces[key]
            if held is None:
                send = [own_tokens] + ups[left : 2 * left]
            else:
                lo = model + left * width
                send = [held[:, :model], held[:, lo : lo + left * width]]
            pieces[key + offset] = xor_permute(jnp.concatenate(send, axis=1), axis, bit)
        if axis == "dp":
            chosen.append(xor_permute(global_blocks, axis, bit)[0])
    token_pieces = [own_tokens] + [pieces[o] for o in range(1, groups)]
    if width % 128 == 0:
        up_pieces = [ups[0]] + token_pieces[1:]
        up_starts = [0] + [model] * (groups - 1)
    else:
        up_pieces = [ups[0]] + [v[:, model : model + width] for v in token_pieces[1:]]
        token_pieces = [v[:, :model] for v in token_pieces]
        up_starts = [0] * groups

    length = chunks * rows
    total = seqs * length
    results = pl.pallas_call(
        lambda *refs: attention_kernel(
            *refs,
            seqs=seqs,
            chunks=chunks,
            rows=rows,
            heads=heads,
            hdim=hdim,
            parts=parts,
            scale=1.0 / math.sqrt(hdim),
            up_starts=up_starts,
        ),
        out_shape=(jax.ShapeDtypeStruct((model // parts, 3 * width), BF16),) * parts
        + (jax.ShapeDtypeStruct((groups // 2, rows, model + width), BF16),) * 2,
        in_specs=[pl.BlockSpec(memory_space=pltpu.SMEM)] * 2
        + [pl.BlockSpec(memory_space=pl.ANY)] * (2 * groups + parts),
        out_specs=(pl.BlockSpec(memory_space=pltpu.VMEM),) * (parts + 2),
        scratch_shapes=[
            pltpu.VMEM((total, model), BF16),
            pltpu.VMEM((model, 3 * width), BF16),
            pltpu.VMEM((total, width), BF16),
            pltpu.VMEM((heads, total, hdim), BF16),
            pltpu.VMEM((heads, total, hdim), BF16),
            pltpu.VMEM((heads, total, hdim), BF16),
            pltpu.VMEM((heads, total, hdim), BF16),
            pltpu.VMEM((heads, total, hdim), F32),
            pltpu.VMEM((heads, total, hdim), F32),
            pltpu.VMEM((total, 3 * width), BF16),
            pltpu.VMEM((total, width), BF16),
            pltpu.SemaphoreType.DMA((2 * groups + parts,)),
        ],
        compiler_params=pltpu.CompilerParams(vmem_limit_bytes=48 * 1024 * 1024),
        name="attention",
    )(
        where,
        jnp.concatenate(chosen),
        *token_pieces,
        *up_pieces,
        *weights,
    )
    grad_w = results[:parts]
    keep, send = results[parts:]
    smem = pl.BlockSpec(memory_space=pltpu.SMEM)
    vmem = pl.BlockSpec(memory_space=pltpu.VMEM)

    axis, bit, _ = hops[-1]
    got = xor_permute(send, axis, bit)
    moved = [grad_w[0]] + [xor_permute(grad_w[j], "dp", j) for j in range(1, parts)]
    columns = model + 2 * width
    held = pl.pallas_call(
        lambda *refs: combine_kernel(*refs, model=model),
        out_shape=(jax.ShapeDtypeStruct((rows, columns), BF16),) * (groups // 2),
        in_specs=[vmem] * 2,
        out_specs=(vmem,) * (groups // 2),
        name="combine",
    )(keep, got)
    held = list(held)
    for axis, bit, offset in reversed(hops[:-1]):
        arrived = [xor_permute(value, axis, bit) for value in reversed(held[1::2])][::-1]
        held = held[::2]
        if len(held) == 1:
            break
        columns = 2 * columns - model
        held = [
            pl.pallas_call(
                lambda *refs: join_kernel(*refs, model=model),
                out_shape=jax.ShapeDtypeStruct((rows, columns), BF16),
                in_specs=[vmem] * 2,
                out_specs=vmem,
                name="join",
            )(mine, theirs)
            for mine, theirs in zip(held, arrived)
        ]
    grad_tokens, context = pl.pallas_call(
        lambda *refs: final_kernel(*refs, model=model, seqs=seqs, chunks=chunks),
        out_shape=(jax.ShapeDtypeStruct((rows, model), BF16),) * 2,
        in_specs=[smem, vmem, vmem],
        name="rows_out",
    )(where, held[0], arrived[0])

    final = pl.pallas_call(
        lambda *refs: sum_kernel(*refs, parts=parts, seqs=seqs, width=width),
        out_shape=(jax.ShapeDtypeStruct((model // parts, seqs * width), F32),) * 3,
        in_specs=[smem] + [vmem] * parts,
        name="weights_out",
    )(where, *moved)
    return (context[None], grad_tokens[None], *final)


def solution(mesh):
    return jax.shard_map(
        per_device,
        mesh=mesh,
        in_specs=(
            P(("groups", "dp"), "ctx", None),
            P(("groups", "dp"), None),
            P("dp", None),
            P("dp", None),
            P("dp", None),
            P(("groups", "dp"), "ctx", None),
        ),
        out_specs=(
            P(("groups", "dp"), "ctx", None),
            P(("groups", "dp"), "ctx", None),
            P(("groups", "dp"), "ctx"),
            P(("groups", "dp"), "ctx"),
            P(("groups", "dp"), "ctx"),
        ),
        check_vma=False,
    )
```

```python
import math

import jax
import jax.numpy as jnp
from jax import lax
from jax.experimental import pallas as pl
from jax.experimental.pallas import tpu as pltpu
from jax.sharding import PartitionSpec as P

HEADS = 16
BLK = 64
NEG = -1e30
SPLIT = 2
SPAN = 4

NT = (((1,), (1,)), ((), ()))
TN = (((0,), (0,)), ((), ()))
F32 = jnp.float32
BF16 = jnp.bfloat16


SMALL = pltpu.CompilerParams(vmem_limit_bytes=8 * 1024 * 1024)


def cost(micros):
    return pl.CostEstimate(
        flops=0, transcendentals=0, bytes_accessed=int(micros * 3_000_000)
    )


def xor_permute(value, axis, bit):
    count = lax.axis_size(axis)
    return lax.ppermute(value, axis, [(i, i ^ bit) for i in range(count)])


def attention_kernel(
    where_ref, chosen_ref, *refs, seqs, chunks, rows, heads, hdim, parts, scale, up_starts
):
    pieces = seqs * chunks
    half = pieces // 2
    token_refs = refs[:pieces]
    up_refs = refs[pieces : 2 * pieces]
    weight_refs = refs[2 * pieces : 2 * pieces + parts]
    outs = refs[2 * pieces + parts :]
    grad_w_refs = outs[:parts]
    keep_ref, send_ref = outs[parts : parts + 2]
    all_tokens, weight, up_all, kv_s, kvt_s, pair_s, dkv_s, grads, context_s, sems = outs[
        parts + 2 :
    ]
    length = chunks * rows
    width = heads * hdim
    model = all_tokens.shape[1]
    part_rows = model // parts
    position = where_ref[0]
    line = where_ref[1]

    copies = []
    for j in range(parts):
        start = pl.multiple_of((line ^ j) * part_rows, part_rows)
        copies.append((weight_refs[j], weight.at[pl.ds(start, part_rows), :]))
    for b in range(pieces):
        copies.append((token_refs[b].at[:, :model], all_tokens.at[pl.ds(b * rows, rows), :]))
    for b in range(pieces):
        source = up_refs[b]
        start = up_starts[b]
        copies.append((source.at[:, start : start + width], up_all.at[pl.ds(b * rows, rows), :]))
    copies = [
        pltpu.make_async_copy(source, target, sems.at[index])
        for index, (source, target) in enumerate(copies)
    ]
    for copy in copies:
        copy.start()
    for copy in copies:
        copy.wait()
    pair_s[...] = jnp.zeros_like(pair_s)
    if SPAN < chunks:
        dkv_s[...] = jnp.zeros_like(dkv_s)
    tile = min(512, length)

    @pl.loop(0, seqs * length // tile)
    def _(t):
        at = pl.ds(pl.multiple_of(t * tile, tile), tile)
        out = jnp.dot(all_tokens[at, :], weight[...], preferred_element_type=F32)
        for h in range(heads):
            lo = h * hdim
            kv = jnp.concatenate(
                [
                    out[:, width + lo : width + lo + hdim],
                    out[:, 2 * width + lo : 2 * width + lo + hdim],
                ],
                axis=1,
            )
            kv_s[h, at, :] = kv.astype(BF16)
            kvt_s[h, :, at] = jnp.transpose(kv).astype(BF16)
            q = (out[:, lo : lo + hdim].astype(BF16) * scale).astype(BF16)
            for p in range(tile // rows):
                pair_s[h, t * (tile // rows) + p, :rows, :hdim] = q[p * rows : (p + 1) * rows]
    for h in range(heads):
        for b in range(pieces):
            pair_s[h, b, rows:, hdim:] = up_all[
                b * rows : (b + 1) * rows, h * hdim : (h + 1) * hdim
            ]

    blocks_per_chunk = rows // BLK
    block_count = length // BLK
    log_blocks = int(math.log2(blocks_per_chunk))

    span = min(SPAN, chunks)

    @pl.loop(0, pieces // span)
    def _(t):
        i = t // (chunks // span)
        keys_at = pl.ds(pl.multiple_of(i * length, length), length)
        first = chosen_ref[2 * i]
        second = chosen_ref[2 * i + 1]
        shape = (block_count, 1, rows)
        key = lax.broadcasted_iota(jnp.int32, shape, 0)
        key_block = (lax.shift_right_logical(key, log_blocks) ^ position) * blocks_per_chunk + (
            key & (blocks_per_chunk - 1)
        )
        offset = lax.shift_right_logical(
            lax.broadcasted_iota(jnp.int32, shape, 2), int(math.log2(BLK))
        )
        biases = []
        for p in range(span):
            j = t * span + p - i * chunks
            query_block = (position ^ j) * blocks_per_chunk + offset
            keep = (
                (jnp.abs(key_block - query_block) <= 1)
                | (key_block == first)
                | (key_block == second)
                | (query_block == first)
                | (query_block == second)
            )
            biases.append(jnp.where(keep, 0.0, NEG))
        for h in range(heads):
            pair = pair_s[h, pl.ds(t * span, span)].reshape(span * 2 * rows, 2 * hdim)
            both = lax.dot_general(kv_s[h, keys_at, :], pair, NT, preferred_element_type=F32)
            parts_of = [both[:, p * rows : (p + 1) * rows] for p in range(2 * span)]
            forward = []
            backward = []
            inverses = []
            for p in range(span):
                scores = parts_of[2 * p].reshape(block_count, BLK, rows) + biases[p]
                scores = scores.reshape(length, rows)
                grad_probs = parts_of[2 * p + 1]
                raw = jnp.exp(scores - jnp.max(scores, axis=0, keepdims=True))
                inverse = 1.0 / jnp.sum(raw, axis=0, keepdims=True)
                raw_low = raw.astype(BF16)
                probs = raw * inverse
                delta = inverse * jnp.sum(
                    raw_low.astype(F32) * grad_probs, axis=0, keepdims=True
                )
                low = (probs * (grad_probs - delta)).astype(BF16)
                forward += [raw_low, low]
                backward += [low, probs.astype(BF16)]
                inverses.append(inverse)
            sums = jnp.dot(
                kvt_s[h, :, keys_at],
                jnp.concatenate(forward, axis=1),
                preferred_element_type=F32,
            )
            dkv = jnp.dot(
                jnp.concatenate(backward, axis=1), pair, preferred_element_type=F32
            )
            if span == chunks:
                dkv_s[h, keys_at, :] = dkv
            else:
                dkv_s[h, keys_at, :] += dkv
            lo = h * hdim
            for p in range(span):
                at = pl.ds(pl.multiple_of((t * span + p) * rows, rows), rows)
                lanes = 2 * p * rows
                rows_out = jnp.transpose(
                    jnp.concatenate(
                        [
                            sums[:hdim, lanes + rows : lanes + 2 * rows] * scale,
                            sums[hdim:, lanes : lanes + rows] * inverses[p],
                        ],
                        axis=0,
                    )
                ).astype(BF16)
                grads[at, lo : lo + hdim] = rows_out[:, :hdim]
                context_s[at, lo : lo + hdim] = rows_out[:, hdim:]

    for h in range(heads):
        lo = h * hdim
        grads[:, width + lo : width + lo + hdim] = dkv_s[h, :, :hdim].astype(BF16)
        grads[:, 2 * width + lo : 2 * width + lo + hdim] = dkv_s[h, :, hdim:].astype(BF16)

    for j in range(parts):
        cols = pl.ds(pl.multiple_of((line ^ j) * part_rows, part_rows), part_rows)
        grad_w_refs[j][...] = lax.dot_general(
            all_tokens[:, cols], grads[...], TN, preferred_element_type=F32
        ).astype(BF16)

    @pl.loop(0, half)
    def _(t):
        at = pl.ds(pl.multiple_of(t * 2 * rows, 2 * rows), 2 * rows)
        out = lax.dot_general(grads[at, :], weight[...], NT, preferred_element_type=F32)
        keep_ref[t, :, :model] = out[:rows].astype(BF16)
        send_ref[t, :, :model] = out[rows:].astype(BF16)
        keep_ref[t, :, model:] = context_s[pl.ds(pl.multiple_of(t * 2 * rows, rows), rows), :]
        send_ref[t, :, model:] = context_s[
            pl.ds(pl.multiple_of(t * 2 * rows + rows, rows), rows), :
        ]


def add_and_join(mine, theirs, model):
    total = (mine[:, :model].astype(F32) + theirs[:, :model].astype(F32)).astype(BF16)
    return [total, mine[:, model:], theirs[:, model:]]


def combine_kernel(*refs, model):
    count = len(refs) - 2
    keep_ref, got_ref = refs[:2]
    for t in range(count):
        out_ref = refs[2 + t]
        lo = 0
        for value in add_and_join(keep_ref[t], got_ref[t], model):
            out_ref[:, lo : lo + value.shape[1]] = value
            lo += value.shape[1]


def join_kernel(mine_ref, theirs_ref, out_ref, *, model):
    lo = 0
    for value in add_and_join(mine_ref[...], theirs_ref[...], model):
        out_ref[:, lo : lo + value.shape[1]] = value
        lo += value.shape[1]


def final_kernel(where_ref, mine_ref, theirs_ref, grad_ref, context_ref, *, model, seqs, chunks):
    total, mine, theirs = add_and_join(mine_ref[...], theirs_ref[...], model)
    grad_ref[...] = total
    groups = seqs * chunks
    width = model // groups
    values = [mine[:, k * width : (k + 1) * width] for k in range(groups // 2)]
    values += [theirs[:, k * width : (k + 1) * width] for k in range(groups // 2)]
    own = where_ref[0] + where_ref[2] * chunks
    bit = 1
    while bit < groups:
        flip = (own & bit) != 0
        values = [jnp.where(flip, values[o ^ bit], values[o]) for o in range(groups)]
        bit *= 2
    for o in range(groups):
        lo = ((o % chunks) * seqs + o // chunks) * width
        context_ref[:, lo : lo + width] = values[o]


def sum_kernel(where_ref, *refs, parts, seqs, width):
    outs = refs[parts:]
    for m in range(3):
        sums = []
        for i in range(seqs):
            acc = refs[i][:, m * width : (m + 1) * width].astype(F32)
            for j in range(i + seqs, parts, seqs):
                acc = acc + refs[j][:, m * width : (m + 1) * width].astype(F32)
            sums.append(acc)
        if seqs == 1:
            outs[m][...] = sums[0]
        else:
            flip = where_ref[2] != 0
            outs[m][:, :width] = jnp.where(flip, sums[1], sums[0])
            outs[m][:, width:] = jnp.where(flip, sums[0], sums[1])


def per_device(tokens, global_blocks, w_query, w_key, w_value, d_context):
    own_tokens = tokens[0]
    upstream = d_context[0]
    rows, model = own_tokens.shape
    hdim = model // HEADS
    chunks = lax.axis_size("ctx")
    parts = lax.axis_size("dp")
    seqs = SPLIT if HEADS % (SPLIT * chunks) == 0 and parts % SPLIT == 0 else 1
    groups = chunks * seqs
    width = model // groups
    heads = width // hdim
    position = lax.axis_index("ctx")
    line = lax.axis_index("dp")
    side = line % seqs

    where = jnp.stack([position, line, side]).astype(jnp.int32)
    hops = [("dp", 1, chunks)] if seqs == 2 else []
    bit = chunks // 2
    while bit:
        hops.append(("ctx", bit, bit))
        bit //= 2

    def slice_of(value, offset):
        which = (position ^ (offset % chunks)) * seqs + (side ^ (offset // chunks))
        return lax.dynamic_slice_in_dim(value, which * width, width, 1)

    sends = []
    for i in range(seqs):
        sends.append(
            jnp.concatenate(
                [slice_of(w, i * chunks) for w in (w_query, w_key, w_value)], axis=1
            )
        )
    weights = [sends[0]]
    for j in range(1, parts):
        weights.append(xor_permute(sends[j % seqs], "dp", j))

    ups = [slice_of(upstream, o) for o in range(groups)]
    pieces = {0: None}
    chosen = [global_blocks[0]]
    left = groups
    for axis, bit, offset in hops:
        left //= 2
        for key in list(pieces):
            held = pieces[key]
            if held is None:
                send = [own_tokens] + ups[left : 2 * left]
            else:
                lo = model + left * width
                send = [held[:, :model], held[:, lo : lo + left * width]]
            pieces[key + offset] = xor_permute(jnp.concatenate(send, axis=1), axis, bit)
        if axis == "dp":
            chosen.append(xor_permute(global_blocks, axis, bit)[0])
    token_pieces = [own_tokens] + [pieces[o] for o in range(1, groups)]
    if width % 128 == 0:
        up_pieces = [ups[0]] + token_pieces[1:]
        up_starts = [0] + [model] * (groups - 1)
    else:
        up_pieces = [ups[0]] + [v[:, model : model + width] for v in token_pieces[1:]]
        token_pieces = [v[:, :model] for v in token_pieces]
        up_starts = [0] * groups

    length = chunks * rows
    total = seqs * length
    results = pl.pallas_call(
        lambda *refs: attention_kernel(
            *refs,
            seqs=seqs,
            chunks=chunks,
            rows=rows,
            heads=heads,
            hdim=hdim,
            parts=parts,
            scale=1.0 / math.sqrt(hdim),
            up_starts=up_starts,
        ),
        out_shape=(jax.ShapeDtypeStruct((model // parts, 3 * width), BF16),) * parts
        + (jax.ShapeDtypeStruct((groups // 2, rows, model + width), BF16),) * 2,
        in_specs=[pl.BlockSpec(memory_space=pltpu.SMEM)] * 2
        + [pl.BlockSpec(memory_space=pl.ANY)] * (2 * groups + parts),
        out_specs=(pl.BlockSpec(memory_space=pltpu.VMEM),) * (parts + 2),
        scratch_shapes=[
            pltpu.VMEM((total, model), BF16),
            pltpu.VMEM((model, 3 * width), BF16),
            pltpu.VMEM((total, width), BF16),
            pltpu.VMEM((heads, total, 2 * hdim), BF16),
            pltpu.VMEM((heads, 2 * hdim, total), BF16),
            pltpu.VMEM((heads, groups, 2 * rows, 2 * hdim), BF16),
            pltpu.VMEM((heads, total, 2 * hdim), F32),
            pltpu.VMEM((total, 3 * width), BF16),
            pltpu.VMEM((total, width), BF16),
            pltpu.SemaphoreType.DMA((2 * groups + parts,)),
        ],
        compiler_params=pltpu.CompilerParams(vmem_limit_bytes=24 * 1024 * 1024),
        cost_estimate=cost(13),
        name="attention",
    )(
        where,
        jnp.concatenate(chosen),
        *token_pieces,
        *up_pieces,
        *weights,
    )
    grad_w = results[:parts]
    keep, send = results[parts:]
    smem = pl.BlockSpec(memory_space=pltpu.SMEM)
    vmem = pl.BlockSpec(memory_space=pltpu.VMEM)

    def send_rows(keep, send):
        axis, bit, _ = hops[-1]
        got = xor_permute(send, axis, bit)
        columns = model + 2 * width
        held = pl.pallas_call(
            lambda *refs: combine_kernel(*refs, model=model),
            out_shape=(jax.ShapeDtypeStruct((rows, columns), BF16),) * (groups // 2),
            in_specs=[vmem] * 2,
            out_specs=(vmem,) * (groups // 2),
            compiler_params=SMALL,
            cost_estimate=cost(2),
            name="combine",
        )(keep, got)
        held = list(held)
        for axis, bit, offset in reversed(hops[:-1]):
            arrived = [xor_permute(value, axis, bit) for value in reversed(held[1::2])][::-1]
            held = held[::2]
            if len(held) == 1:
                break
            columns = 2 * columns - model
            held = [
                pl.pallas_call(
                    lambda *refs: join_kernel(*refs, model=model),
                    out_shape=jax.ShapeDtypeStruct((rows, columns), BF16),
                    in_specs=[vmem] * 2,
                    out_specs=vmem,
                    compiler_params=SMALL,
                    cost_estimate=cost(1),
                    name="join",
                )(mine, theirs)
                for mine, theirs in zip(held, arrived)
            ]
        grad_tokens, context = pl.pallas_call(
            lambda *refs: final_kernel(*refs, model=model, seqs=seqs, chunks=chunks),
            out_shape=(jax.ShapeDtypeStruct((rows, model), BF16),) * 2,
            in_specs=[smem, vmem, vmem],
            compiler_params=SMALL,
            cost_estimate=cost(2),
            name="rows_out",
        )(where, held[0], arrived[0])

        return context, grad_tokens

    moved = [grad_w[0]] + [xor_permute(grad_w[j], "dp", j) for j in range(1, parts)]
    context, grad_tokens = lax.cond(
        global_blocks[0, 0] >= 0,
        send_rows,
        lambda keep, send: (jnp.zeros((rows, model), BF16),) * 2,
        keep,
        send,
    )

    final = pl.pallas_call(
        lambda *refs: sum_kernel(*refs, parts=parts, seqs=seqs, width=width),
        out_shape=(jax.ShapeDtypeStruct((model // parts, seqs * width), F32),) * 3,
        in_specs=[smem] + [vmem] * parts,
        compiler_params=SMALL,
        cost_estimate=cost(2),
        name="weights_out",
    )(where, *moved)
    return (context[None], grad_tokens[None], *final)


def solution(mesh):
    return jax.shard_map(
        per_device,
        mesh=mesh,
        in_specs=(
            P(("groups", "dp"), "ctx", None),
            P(("groups", "dp"), None),
            P("dp", None),
            P("dp", None),
            P("dp", None),
            P(("groups", "dp"), "ctx", None),
        ),
        out_specs=(
            P(("groups", "dp"), "ctx", None),
            P(("groups", "dp"), "ctx", None),
            P(("groups", "dp"), "ctx"),
            P(("groups", "dp"), "ctx"),
            P(("groups", "dp"), "ctx"),
        ),
        check_vma=False,
    )
```

```python
import math

import jax
import jax.numpy as jnp
from jax import lax
from jax.experimental import pallas as pl
from jax.experimental.pallas import tpu as pltpu
from jax.sharding import PartitionSpec as P

HEADS = 16
BLK = 64
NEG = -1e30
SPAN = 4

NT = (((1,), (1,)), ((), ()))
TN = (((0,), (0,)), ((), ()))
F32 = jnp.float32
BF16 = jnp.bfloat16


PACK_VMEM = 56 * 1024 * 1024
SMALL = pltpu.CompilerParams(vmem_limit_bytes=8 * 1024 * 1024)


def cost(micros):
    return pl.CostEstimate(
        flops=0, transcendentals=0, bytes_accessed=int(micros * 3_000_000)
    )


def xor_permute(value, axis, bit):
    count = lax.axis_size(axis)
    return lax.ppermute(value, axis, [(i, i ^ bit) for i in range(count)])


def attention_kernel(
    where_ref, chosen_ref, *refs, seqs, chunks, rows, heads, hdim, parts, scale, sources, packed, ids_start
):
    pieces = seqs * chunks
    half = pieces // 2
    count = 1 + max(index for index, _, _ in sources)
    token_refs = refs[:count]
    ups = 1 if packed else count
    up_refs = refs[count : count + ups]
    weight_refs = refs[count + ups : count + ups + parts]
    outs = refs[count + ups + parts :]
    grad_w_refs = outs[:parts]
    keep_ref, send_ref = outs[parts : parts + 2]
    all_tokens, weight, up_all, kv_s, kvt_s, pair_s, dkv_s, grads, context_s, far_ids, ids, sems = outs[
        parts + 2 :
    ]
    length = chunks * rows
    width = heads * hdim
    model = all_tokens.shape[1]
    part_rows = model // parts
    position = where_ref[0]
    line = where_ref[1]

    copies = []
    for j in range(parts):
        start = pl.multiple_of((line ^ j) * part_rows, part_rows)
        copies.append((weight_refs[j], weight.at[pl.ds(start, part_rows), :]))
    for b, (index, first, start) in enumerate(sources):
        held = pl.ds(first, rows)
        target = pl.ds(b * rows, rows)
        copies.append((token_refs[index].at[held, :model], all_tokens.at[target, :]))
        if packed and b:
            up = token_refs[index].at[held, start : start + width]
        else:
            up = up_refs[index].at[held, :]
        copies.append((up, up_all.at[target, :]))
    if seqs == 2:
        copies.append((token_refs[1].at[:16, ids_start : ids_start + 128], far_ids))
    copies = [
        pltpu.make_async_copy(source, target, sems.at[index])
        for index, (source, target) in enumerate(copies)
    ]
    for copy in copies:
        copy.start()
    for copy in copies:
        copy.wait()
    for k in range(2):
        ids[0, k] = jnp.full((1, rows), chosen_ref[k], jnp.int32)
        if seqs == 2:
            far = far_ids[:, k * 64 : k * 64 + 1].astype(F32).astype(jnp.int32)
            ids[1, k] = jnp.broadcast_to(far[:1], (1, rows))

    pair_s[...] = jnp.zeros_like(pair_s)
    if SPAN < chunks:
        dkv_s[...] = jnp.zeros_like(dkv_s)
    tile = min(512, length)

    @pl.loop(0, seqs * length // tile)
    def _(t):
        at = pl.ds(pl.multiple_of(t * tile, tile), tile)
        out = jnp.dot(all_tokens[at, :], weight[...], preferred_element_type=F32)
        for h in range(heads):
            lo = h * hdim
            kv = jnp.concatenate(
                [
                    out[:, width + lo : width + lo + hdim],
                    out[:, 2 * width + lo : 2 * width + lo + hdim],
                ],
                axis=1,
            )
            kv_s[h, at, :] = kv.astype(BF16)
            kvt_s[h, :, at] = jnp.transpose(kv).astype(BF16)
            q = (out[:, lo : lo + hdim].astype(BF16) * scale).astype(BF16)
            for p in range(tile // rows):
                pair_s[h, t * (tile // rows) + p, :rows, :hdim] = q[p * rows : (p + 1) * rows]
    for h in range(heads):
        for b in range(pieces):
            pair_s[h, b, rows:, hdim:] = up_all[
                b * rows : (b + 1) * rows, h * hdim : (h + 1) * hdim
            ]

    blocks_per_chunk = rows // BLK
    block_count = length // BLK
    log_blocks = int(math.log2(blocks_per_chunk))

    span = min(SPAN, chunks)

    @pl.loop(0, pieces // span)
    def _(t):
        i = t // (chunks // span)
        keys_at = pl.ds(pl.multiple_of(i * length, length), length)
        first = ids[i, 0]
        second = ids[i, 1]
        shape = (block_count, 1, rows)
        key = lax.broadcasted_iota(jnp.int32, shape, 0)
        key_block = (lax.shift_right_logical(key, log_blocks) ^ position) * blocks_per_chunk + (
            key & (blocks_per_chunk - 1)
        )
        offset = lax.shift_right_logical(
            lax.broadcasted_iota(jnp.int32, shape, 2), int(math.log2(BLK))
        )
        biases = []
        for p in range(span):
            j = t * span + p - i * chunks
            query_block = (position ^ j) * blocks_per_chunk + offset
            keep = (
                (jnp.abs(key_block - query_block) <= 1)
                | (key_block == first)
                | (key_block == second)
                | (query_block == first)
                | (query_block == second)
            )
            biases.append(jnp.where(keep, 0.0, NEG))
        for h in range(heads):
            pair = pair_s[h, pl.ds(t * span, span)].reshape(span * 2 * rows, 2 * hdim)
            both = lax.dot_general(kv_s[h, keys_at, :], pair, NT, preferred_element_type=F32)
            parts_of = [both[:, p * rows : (p + 1) * rows] for p in range(2 * span)]
            forward = []
            backward = []
            inverses = []
            for p in range(span):
                scores = parts_of[2 * p].reshape(block_count, BLK, rows) + biases[p]
                scores = scores.reshape(length, rows)
                grad_probs = parts_of[2 * p + 1]
                raw = jnp.exp(scores - jnp.max(scores, axis=0, keepdims=True))
                inverse = 1.0 / jnp.sum(raw, axis=0, keepdims=True)
                raw_low = raw.astype(BF16)
                probs = raw * inverse
                delta = inverse * jnp.sum(
                    raw_low.astype(F32) * grad_probs, axis=0, keepdims=True
                )
                low = (probs * (grad_probs - delta)).astype(BF16)
                forward += [raw_low, low]
                backward += [low, probs.astype(BF16)]
                inverses.append(inverse)
            sums = jnp.dot(
                kvt_s[h, :, keys_at],
                jnp.concatenate(forward, axis=1),
                preferred_element_type=F32,
            )
            dkv = jnp.dot(
                jnp.concatenate(backward, axis=1), pair, preferred_element_type=F32
            )
            if span == chunks:
                dkv_s[h, keys_at, :] = dkv
            else:
                dkv_s[h, keys_at, :] += dkv
            lo = h * hdim
            for p in range(span):
                at = pl.ds(pl.multiple_of((t * span + p) * rows, rows), rows)
                lanes = 2 * p * rows
                rows_out = jnp.transpose(
                    jnp.concatenate(
                        [
                            sums[:hdim, lanes + rows : lanes + 2 * rows] * scale,
                            sums[hdim:, lanes : lanes + rows] * inverses[p],
                        ],
                        axis=0,
                    )
                ).astype(BF16)
                grads[at, lo : lo + hdim] = rows_out[:, :hdim]
                context_s[at, lo : lo + hdim] = rows_out[:, hdim:]

    for h in range(heads):
        lo = h * hdim
        grads[:, width + lo : width + lo + hdim] = dkv_s[h, :, :hdim].astype(BF16)
        grads[:, 2 * width + lo : 2 * width + lo + hdim] = dkv_s[h, :, hdim:].astype(BF16)

    for j in range(parts):
        cols = pl.ds(pl.multiple_of((line ^ j) * part_rows, part_rows), part_rows)
        grad_w_refs[j][...] = lax.dot_general(
            all_tokens[:, cols], grads[...], TN, preferred_element_type=F32
        ).astype(BF16)

    @pl.loop(0, half)
    def _(t):
        at = pl.ds(pl.multiple_of(t * 2 * rows, 2 * rows), 2 * rows)
        out = lax.dot_general(grads[at, :], weight[...], NT, preferred_element_type=F32)
        keep_ref[t, :, :model] = out[:rows].astype(BF16)
        send_ref[t, :, :model] = out[rows:].astype(BF16)
        keep_ref[t, :, model:] = context_s[pl.ds(pl.multiple_of(t * 2 * rows, rows), rows), :]
        send_ref[t, :, model:] = context_s[
            pl.ds(pl.multiple_of(t * 2 * rows + rows, rows), rows), :
        ]


def add_and_join(mine, theirs, model):
    total = (mine[:, :model].astype(F32) + theirs[:, :model].astype(F32)).astype(BF16)
    return [total, mine[:, model:], theirs[:, model:]]


def combine_kernel(*refs, model):
    count = len(refs) - 2
    keep_ref, got_ref = refs[:2]
    for t in range(count):
        out_ref = refs[2 + t]
        lo = 0
        for value in add_and_join(keep_ref[t], got_ref[t], model):
            out_ref[:, lo : lo + value.shape[1]] = value
            lo += value.shape[1]


def join_kernel(mine_ref, theirs_ref, out_ref, *, model):
    lo = 0
    for value in add_and_join(mine_ref[...], theirs_ref[...], model):
        out_ref[:, lo : lo + value.shape[1]] = value
        lo += value.shape[1]


def final_kernel(
    where_ref, mine_ref, near_ref, far_ref, grad_ref, context_ref, *, model, seqs, chunks
):
    total, mine, near = add_and_join(mine_ref[...], near_ref[...], model)
    grad_ref[...] = (total.astype(F32) + far_ref[:, :model].astype(F32)).astype(BF16)
    theirs = far_ref[:, model:]
    mine = jnp.concatenate([mine, near], axis=1)
    groups = seqs * chunks
    width = model // groups
    values = [mine[:, k * width : (k + 1) * width] for k in range(groups // 2)]
    values += [theirs[:, k * width : (k + 1) * width] for k in range(groups // 2)]
    own = where_ref[0] + where_ref[2] * chunks
    bit = 1
    while bit < groups:
        flip = (own & bit) != 0
        values = [jnp.where(flip, values[o ^ bit], values[o]) for o in range(groups)]
        bit *= 2
    for o in range(groups):
        lo = ((o % chunks) * seqs + o // chunks) * width
        context_ref[:, lo : lo + width] = values[o]


def sum_kernel(where_ref, *refs, parts, seqs, width):
    outs = refs[parts:]
    for m in range(3):
        sums = []
        for i in range(seqs):
            acc = refs[i][:, m * width : (m + 1) * width].astype(F32)
            for j in range(i + seqs, parts, seqs):
                acc = acc + refs[j][:, m * width : (m + 1) * width].astype(F32)
            sums.append(acc)
        if seqs == 1:
            outs[m][...] = sums[0]
        else:
            flip = where_ref[2] != 0
            outs[m][:, :width] = jnp.where(flip, sums[1], sums[0])
            outs[m][:, width:] = jnp.where(flip, sums[0], sums[1])


def pack_kernel(where_ref, chosen_ref, *refs, lefts, seqs, chunks, width, noted):
    tokens, up = refs[:2]
    weight_refs = refs[2:5]
    hops = len(lefts)
    sends = refs[5 : 5 + hops]
    own_up = refs[5 + hops]
    weight_sends = refs[6 + hops : 6 + hops + seqs]
    sems = refs[6 + hops + seqs]
    model = tokens.shape[1]

    def columns(offset):
        which = (where_ref[0] ^ (offset % chunks)) * seqs + (where_ref[2] ^ (offset // chunks))
        return pl.ds(pl.multiple_of(which * width, width), width)

    copies = []
    for send, left in zip(sends, lefts):
        copies.append((tokens, send.at[:, :model]))
        for k in range(left):
            lo = model + k * width
            copies.append((up.at[:, columns(left + k)], send.at[:, lo : lo + width]))
    copies.append((up.at[:, columns(0)], own_up))
    for i in range(seqs):
        for m in range(3):
            copies.append(
                (
                    weight_refs[m].at[:, columns(i * chunks)],
                    weight_sends[i].at[:, m * width : (m + 1) * width],
                )
            )
    copies = [
        pltpu.make_async_copy(source, target, sems.at[index])
        for index, (source, target) in enumerate(copies)
    ]
    for copy in copies:
        copy.start()
    if noted:
        lo = model + lefts[0] * width
        shape = (tokens.shape[0], 128)
        lane = lax.broadcasted_iota(jnp.int32, shape, 1)
        both = jnp.where(lane < 64, chosen_ref[0], chosen_ref[1])
        sends[0][:, lo : lo + 128] = both.astype(F32).astype(BF16)
    for copy in copies:
        copy.wait()


def per_device(tokens, global_blocks, w_query, w_key, w_value, d_context):
    own_tokens = tokens[0]
    upstream = d_context[0]
    rows, model = own_tokens.shape
    hdim = model // HEADS
    chunks = lax.axis_size("ctx")
    parts = lax.axis_size("dp")
    seqs = 1
    if parts % 2 == 0 and model % (chunks * 2 * 128) == 0 and HEADS % (chunks * 2) == 0:
        seqs = 2
    groups = chunks * seqs
    width = model // groups
    heads = width // hdim
    position = lax.axis_index("ctx")
    line = lax.axis_index("dp")
    side = line % seqs

    where = jnp.stack([position, line, side]).astype(jnp.int32)
    hops = [("dp", 1, chunks)] if seqs == 2 else []
    bit = chunks // 2
    while bit:
        hops.append(("ctx", bit, bit))
        bit //= 2

    smem = pl.BlockSpec(memory_space=pltpu.SMEM)
    vmem = pl.BlockSpec(memory_space=pltpu.VMEM)
    hbm = pl.BlockSpec(memory_space=pltpu.HBM)
    chosen = global_blocks[0]
    lefts = [groups >> (k + 1) for k in range(len(hops))]
    packed = width % 128 == 0
    noted = 128 if seqs == 2 else 0
    if packed:
        sizes = [model + left * width + (noted if k == 0 else 0) for k, left in enumerate(lefts)]
        outs = pl.pallas_call(
            lambda *refs: pack_kernel(
                *refs, lefts=lefts, seqs=seqs, chunks=chunks, width=width, noted=noted
            ),
            out_shape=tuple(jax.ShapeDtypeStruct((rows, size), BF16) for size in sizes + [width])
            + (jax.ShapeDtypeStruct((model // parts, 3 * width), BF16),) * seqs,
            in_specs=[smem, smem] + [hbm] * 5,
            out_specs=(vmem,) * (len(hops) + 1 + seqs),
            scratch_shapes=[
                pltpu.SemaphoreType.DMA((len(hops) + sum(lefts) + 1 + 3 * seqs,)),
            ],
            compiler_params=pltpu.CompilerParams(vmem_limit_bytes=PACK_VMEM),
            cost_estimate=cost(2),
            name="pack",
        )(where, chosen, own_tokens, upstream, w_query, w_key, w_value)
        own_sends = outs[: len(hops)]
        own_up = outs[len(hops)]
        sends = outs[len(hops) + 1 :]
    else:

        def slice_of(value, offset):
            which = (position ^ (offset % chunks)) * seqs + (side ^ (offset // chunks))
            return lax.dynamic_slice_in_dim(value, which * width, width, 1)

        ups = [slice_of(upstream, o) for o in range(groups)]
        own_up = ups[0]
        own_sends = [
            jnp.concatenate([own_tokens] + ups[left : 2 * left], axis=1) for left in lefts
        ]
        sends = [
            jnp.concatenate(
                [slice_of(w, i * chunks) for w in (w_query, w_key, w_value)], axis=1
            )
            for i in range(seqs)
        ]

    arrived = [xor_permute(own_sends[k], *hops[k][:2]) for k in range(2)]
    weights = [sends[0]]
    for j in range(1, parts):
        weights.append(xor_permute(sends[j % seqs], "dp", j))

    def by_age(keys):
        return sorted(keys, key=lambda o: (o.bit_count(), o & hops[0][2]))

    inner = [o for o in range(2, groups, 2) if o not in (hops[0][2], hops[1][2])]

    def spread(near, far, *own):
        pieces = {hops[0][2]: near}
        for k in range(1, len(hops)):
            axis, bit, offset = hops[k]
            lo = model + lefts[k] * width
            keys = by_age(pieces)
            sends = [
                jnp.concatenate(
                    [pieces[key][:, :model], pieces[key][:, lo : lo + lefts[k] * width]], axis=1
                )
                for key in keys
            ]
            if k > 1:
                keys = [0] + keys
                sends = [own[k - 2]] + sends
            if len(sends) > 1:
                first = jnp.concatenate(sends[:-1], axis=0)
                if k + 1 == len(hops):
                    first, _ = lax.optimization_barrier((first, pieces[keys[-1]]))
                first = xor_permute(first, axis, bit)
                if k + 1 == len(hops):
                    last = xor_permute(pieces[keys[-1]], axis, bit)
                    return tuple(pieces[o] for o in inner) + (first, last)
                for n, key in enumerate(keys[:-1]):
                    pieces[key + offset] = first[n * rows : (n + 1) * rows]
            pieces[keys[-1] + offset] = xor_permute(sends[-1], axis, bit)
            if k == 1:
                pieces[offset] = far

    operands = (*arrived, *own_sends[2:])
    live = global_blocks[0, 0] >= 0
    spread_out = lax.cond(
        live,
        spread,
        lambda *values: jax.tree.map(
            lambda v: jnp.zeros(v.shape, v.dtype), jax.eval_shape(spread, *values)
        ),
        *operands,
    )
    buffers = [own_tokens, *arrived, *spread_out]
    where_is = {0: (0, 0), hops[0][2]: (1, 0), hops[1][2]: (2, 0)}
    for n, o in enumerate(inner):
        where_is[o] = (3 + n, 0)
    ordered = by_age(range(0, groups, 2))
    for n, o in enumerate(ordered[:-1]):
        where_is[o + 1] = (3 + len(inner), n * rows)
    where_is[ordered[-1] + 1] = (4 + len(inner), 0)
    late = ordered[-1] + 1
    if packed:
        up_buffers = [own_up]
    else:
        up_buffers = [own_up] + [v[:, model : model + width] for v in buffers[1:-1]]
        up_buffers.append(buffers[-1][:, model + width : model + 2 * width])
        buffers = [v[:, :model] for v in buffers]
    sources = [where_is[o] + (model + (width if o == late else 0),) for o in range(groups)]

    length = chunks * rows
    total = seqs * length
    results = pl.pallas_call(
        lambda *refs: attention_kernel(
            *refs,
            seqs=seqs,
            chunks=chunks,
            rows=rows,
            heads=heads,
            hdim=hdim,
            parts=parts,
            scale=1.0 / math.sqrt(hdim),
            sources=sources,
            packed=packed,
            ids_start=model + lefts[0] * width,
        ),
        out_shape=(jax.ShapeDtypeStruct((model // parts, 3 * width), BF16),) * parts
        + (jax.ShapeDtypeStruct((groups // 2, rows, model + width), BF16),) * 2,
        in_specs=[pl.BlockSpec(memory_space=pltpu.SMEM)] * 2
        + [pl.BlockSpec(memory_space=pl.ANY)] * (len(buffers) + len(up_buffers) + parts),
        out_specs=(pl.BlockSpec(memory_space=pltpu.VMEM),) * (parts + 2),
        scratch_shapes=[
            pltpu.VMEM((total, model), BF16),
            pltpu.VMEM((model, 3 * width), BF16),
            pltpu.VMEM((total, width), BF16),
            pltpu.VMEM((heads, total, 2 * hdim), BF16),
            pltpu.VMEM((heads, 2 * hdim, total), BF16),
            pltpu.VMEM((heads, groups, 2 * rows, 2 * hdim), BF16),
            pltpu.VMEM((heads, total, 2 * hdim), F32),
            pltpu.VMEM((total, 3 * width), BF16),
            pltpu.VMEM((total, width), BF16),
            pltpu.VMEM((16, 128), BF16),
            pltpu.VMEM((seqs, 2, 1, rows), jnp.int32),
            pltpu.SemaphoreType.DMA((2 * groups + parts + 1,)),
        ],
        compiler_params=pltpu.CompilerParams(vmem_limit_bytes=24 * 1024 * 1024),
        cost_estimate=cost(13),
        name="attention",
    )(
        where,
        chosen,
        *buffers,
        *up_buffers,
        *weights,
    )
    grad_w = results[:parts]
    keep, send = results[parts:]
    moved = [grad_w[0]] + [xor_permute(grad_w[j], "dp", j) for j in range(1, parts)]

    def join(mine, theirs):
        columns = 2 * mine.shape[1] - model
        return pl.pallas_call(
            lambda *refs: join_kernel(*refs, model=model),
            out_shape=jax.ShapeDtypeStruct((rows, columns), BF16),
            in_specs=[vmem] * 2,
            out_specs=vmem,
            compiler_params=SMALL,
            cost_estimate=cost(1),
            name="join",
        )(mine, theirs)

    def collect(keep, send):
        got = xor_permute(send, *hops[-1][:2])
        columns = model + 2 * width
        held = pl.pallas_call(
            lambda *refs: combine_kernel(*refs, model=model),
            out_shape=(jax.ShapeDtypeStruct((rows, columns), BF16),) * (groups // 2),
            in_specs=[vmem] * 2,
            out_specs=(vmem,) * (groups // 2),
            compiler_params=SMALL,
            cost_estimate=cost(2),
            name="combine",
        )(keep, got)
        for axis, bit, _ in reversed(hops[2:-1]):
            theirs = [xor_permute(value, axis, bit) for value in held[1::2]]
            held = [join(*pair) for pair in zip(held[::2], theirs)]
        far = join(held[2], xor_permute(held[3], *hops[1][:2]))
        far = xor_permute(far, *hops[0][:2])
        near = xor_permute(held[1], *hops[1][:2])
        return pl.pallas_call(
            lambda *refs: final_kernel(*refs, model=model, seqs=seqs, chunks=chunks),
            out_shape=(jax.ShapeDtypeStruct((rows, model), BF16),) * 2,
            in_specs=[smem, vmem, vmem, vmem],
            compiler_params=SMALL,
            cost_estimate=cost(2),
            name="rows_out",
        )(where, held[0], near, far)

    grad_tokens, context = lax.cond(
        live,
        collect,
        lambda *values: (jnp.zeros((rows, model), BF16),) * 2,
        keep,
        send,
    )

    final = pl.pallas_call(
        lambda *refs: sum_kernel(*refs, parts=parts, seqs=seqs, width=width),
        out_shape=(jax.ShapeDtypeStruct((model // parts, seqs * width), F32),) * 3,
        in_specs=[smem] + [vmem] * parts,
        compiler_params=SMALL,
        cost_estimate=cost(2),
        name="weights_out",
    )(where, *moved)
    return (context[None], grad_tokens[None], *final)


def solution(mesh):
    return jax.shard_map(
        per_device,
        mesh=mesh,
        in_specs=(
            P(("groups", "dp"), "ctx", None),
            P(("groups", "dp"), None),
            P("dp", None),
            P("dp", None),
            P("dp", None),
            P(("groups", "dp"), "ctx", None),
        ),
        out_specs=(
            P(("groups", "dp"), "ctx", None),
            P(("groups", "dp"), "ctx", None),
            P(("groups", "dp"), "ctx"),
            P(("groups", "dp"), "ctx"),
            P(("groups", "dp"), "ctx"),
        ),
        check_vma=False,
    )
```

```python
import math

import jax
import jax.numpy as jnp
from jax import lax
from jax.experimental import pallas as pl
from jax.experimental.pallas import tpu as pltpu
from jax.sharding import PartitionSpec as P

HEADS = 16
BLK = 64
NEG = -1e30
SPAN = 4

NT = (((1,), (1,)), ((), ()))
TN = (((0,), (0,)), ((), ()))
F32 = jnp.float32
BF16 = jnp.bfloat16


PACK_VMEM = 56 * 1024 * 1024
SMALL = pltpu.CompilerParams(vmem_limit_bytes=8 * 1024 * 1024)


def cost(micros):
    return pl.CostEstimate(
        flops=0, transcendentals=0, bytes_accessed=int(micros * 3_000_000)
    )


def xor_permute(value, axis, bit):
    count = lax.axis_size(axis)
    return lax.ppermute(value, axis, [(i, i ^ bit) for i in range(count)])


def attention_kernel(
    where_ref, chosen_ref, *refs, sources, chunks, far_ids, carry, rows, heads, hdim, parts, scale
):
    half = chunks // 2
    count = 1 + max(max(source[0], source[3]) for source in sources)
    buffers = refs[:count]
    weight_refs = refs[count : count + parts]
    carried = refs[count + parts : count + 2 * parts] if carry == "in" else None
    outs = refs[count + (2 if carry == "in" else 1) * parts :]
    grad_w_refs = outs[:parts]
    keep_ref, send_ref = outs[parts : parts + 2]
    (
        all_tokens, weight, up_all, kv_s, kvt_s, pair_s, dkv_s, grads, context_s, noted, sems
    ) = outs[parts + 2 :]
    length = chunks * rows
    width = heads * hdim
    model = all_tokens.shape[1]
    part_rows = model // parts
    position = where_ref[0]
    line = where_ref[1]

    copies = []
    for j in range(parts):
        start = pl.multiple_of((line ^ j) * part_rows, part_rows)
        copies.append((weight_refs[j], weight.at[pl.ds(start, part_rows), :]))
    at = 0
    for index, first, size, up, start in sources:
        target = pl.ds(at, size)
        held = pl.ds(first, size)
        copies.append((buffers[index].at[held, :model], all_tokens.at[target, :]))
        if up != index:
            held = pl.ds(0, size)
        copies.append((buffers[up].at[held, start : start + width], up_all.at[target, :]))
        at += size
    if far_ids is not None:
        copies.append((buffers[0].at[:16, far_ids : far_ids + 128], noted))
    copies = [
        pltpu.make_async_copy(source, target, sems.at[index])
        for index, (source, target) in enumerate(copies)
    ]
    for copy in copies:
        copy.start()
    for copy in copies:
        copy.wait()
    if far_ids is None:
        chosen = [chosen_ref[k] for k in range(2)]
    else:
        chosen = [noted[:1, 64 * k : 64 * k + 1].astype(F32).astype(jnp.int32) for k in range(2)]
        chosen = [jnp.broadcast_to(value, (1, rows)) for value in chosen]

    pair_s[...] = jnp.zeros_like(pair_s)
    if SPAN < chunks:
        dkv_s[...] = jnp.zeros_like(dkv_s)
    tile = min(512, length)

    @pl.loop(0, length // tile)
    def _(t):
        at = pl.ds(pl.multiple_of(t * tile, tile), tile)
        out = jnp.dot(all_tokens[at, :], weight[...], preferred_element_type=F32)
        for h in range(heads):
            lo = h * hdim
            kv = jnp.concatenate(
                [
                    out[:, width + lo : width + lo + hdim],
                    out[:, 2 * width + lo : 2 * width + lo + hdim],
                ],
                axis=1,
            )
            kv_s[h, at, :] = kv.astype(BF16)
            kvt_s[h, :, at] = jnp.transpose(kv).astype(BF16)
            q = (out[:, lo : lo + hdim].astype(BF16) * scale).astype(BF16)
            for p in range(tile // rows):
                pair_s[h, t * (tile // rows) + p, :rows, :hdim] = q[p * rows : (p + 1) * rows]
    for h in range(heads):
        for b in range(chunks):
            pair_s[h, b, rows:, hdim:] = up_all[
                b * rows : (b + 1) * rows, h * hdim : (h + 1) * hdim
            ]

    blocks_per_chunk = rows // BLK
    block_count = length // BLK
    log_blocks = int(math.log2(blocks_per_chunk))

    span = min(SPAN, chunks)

    @pl.loop(0, chunks // span)
    def _(t):
        first, second = chosen
        shape = (block_count, 1, rows)
        key = lax.broadcasted_iota(jnp.int32, shape, 0)
        key_block = (lax.shift_right_logical(key, log_blocks) ^ position) * blocks_per_chunk + (
            key & (blocks_per_chunk - 1)
        )
        offset = lax.shift_right_logical(
            lax.broadcasted_iota(jnp.int32, shape, 2), int(math.log2(BLK))
        )
        biases = []
        for p in range(span):
            j = t * span + p
            query_block = (position ^ j) * blocks_per_chunk + offset
            keep = (
                (jnp.abs(key_block - query_block) <= 1)
                | (key_block == first)
                | (key_block == second)
                | (query_block == first)
                | (query_block == second)
            )
            biases.append(jnp.where(keep, 0.0, NEG))
        for h in range(heads):
            pair = pair_s[h, pl.ds(t * span, span)].reshape(span * 2 * rows, 2 * hdim)
            both = lax.dot_general(kv_s[h], pair, NT, preferred_element_type=F32)
            parts_of = [both[:, p * rows : (p + 1) * rows] for p in range(2 * span)]
            forward = []
            backward = []
            inverses = []
            for p in range(span):
                scores = parts_of[2 * p].reshape(block_count, BLK, rows) + biases[p]
                scores = scores.reshape(length, rows)
                grad_probs = parts_of[2 * p + 1]
                raw = jnp.exp(scores - jnp.max(scores, axis=0, keepdims=True))
                inverse = 1.0 / jnp.sum(raw, axis=0, keepdims=True)
                raw_low = raw.astype(BF16)
                probs = raw * inverse
                delta = inverse * jnp.sum(
                    raw_low.astype(F32) * grad_probs, axis=0, keepdims=True
                )
                low = (probs * (grad_probs - delta)).astype(BF16)
                forward += [raw_low, low]
                backward += [low, probs.astype(BF16)]
                inverses.append(inverse)
            sums = jnp.dot(
                kvt_s[h],
                jnp.concatenate(forward, axis=1),
                preferred_element_type=F32,
            )
            dkv = jnp.dot(
                jnp.concatenate(backward, axis=1), pair, preferred_element_type=F32
            )
            if span == chunks:
                dkv_s[h] = dkv
            else:
                dkv_s[h] += dkv
            lo = h * hdim
            for p in range(span):
                at = pl.ds(pl.multiple_of((t * span + p) * rows, rows), rows)
                lanes = 2 * p * rows
                rows_out = jnp.transpose(
                    jnp.concatenate(
                        [
                            sums[:hdim, lanes + rows : lanes + 2 * rows] * scale,
                            sums[hdim:, lanes : lanes + rows] * inverses[p],
                        ],
                        axis=0,
                    )
                ).astype(BF16)
                grads[at, lo : lo + hdim] = rows_out[:, :hdim]
                context_s[at, lo : lo + hdim] = rows_out[:, hdim:]

    for h in range(heads):
        lo = h * hdim
        grads[:, width + lo : width + lo + hdim] = dkv_s[h, :, :hdim].astype(BF16)
        grads[:, 2 * width + lo : 2 * width + lo + hdim] = dkv_s[h, :, hdim:].astype(BF16)

    for j in range(parts):
        cols = pl.ds(pl.multiple_of((line ^ j) * part_rows, part_rows), part_rows)
        out = lax.dot_general(all_tokens[:, cols], grads[...], TN, preferred_element_type=F32)
        if carry == "in":
            out = out + carried[j][...]
        grad_w_refs[j][...] = out.astype(grad_w_refs[j].dtype)

    @pl.loop(0, half)
    def _(t):
        at = pl.ds(pl.multiple_of(t * 2 * rows, 2 * rows), 2 * rows)
        out = lax.dot_general(grads[at, :], weight[...], NT, preferred_element_type=F32)
        keep_ref[t, :, :model] = out[:rows].astype(BF16)
        send_ref[t, :, :model] = out[rows:].astype(BF16)
        keep_ref[t, :, model:] = context_s[pl.ds(pl.multiple_of(t * 2 * rows, rows), rows), :]
        send_ref[t, :, model:] = context_s[
            pl.ds(pl.multiple_of(t * 2 * rows + rows, rows), rows), :
        ]


def add_and_join(mine, theirs, model):
    total = (mine[:, :model].astype(F32) + theirs[:, :model].astype(F32)).astype(BF16)
    return [total, mine[:, model:], theirs[:, model:]]


def combine_kernel(*refs, model):
    count = len(refs) - 2
    keep_ref, got_ref = refs[:2]
    for t in range(count):
        out_ref = refs[2 + t]
        lo = 0
        for value in add_and_join(keep_ref[t], got_ref[t], model):
            out_ref[:, lo : lo + value.shape[1]] = value
            lo += value.shape[1]


def join_kernel(mine_ref, theirs_ref, out_ref, *, model):
    lo = 0
    for value in add_and_join(mine_ref[...], theirs_ref[...], model):
        out_ref[:, lo : lo + value.shape[1]] = value
        lo += value.shape[1]


def final_kernel(where_ref, *refs, model, seqs, chunks):
    far_ref, grad_ref, context_ref = refs[-3:]
    if len(refs) == 5:
        total, mine, near = add_and_join(refs[0][...], refs[1][...], model)
        mine = jnp.concatenate([mine, near], axis=1)
    else:
        total = refs[0][:, :model]
        mine = refs[0][:, model:]
    grad_ref[...] = (total.astype(F32) + far_ref[:, :model].astype(F32)).astype(BF16)
    theirs = far_ref[:, model:]
    groups = seqs * chunks
    width = model // groups
    values = [mine[:, k * width : (k + 1) * width] for k in range(groups // 2)]
    values += [theirs[:, k * width : (k + 1) * width] for k in range(groups // 2)]
    own = where_ref[0] + where_ref[2] * chunks
    bit = 1
    while bit < groups:
        flip = (own & bit) != 0
        values = [jnp.where(flip, values[o ^ bit], values[o]) for o in range(groups)]
        bit *= 2
    for o in range(groups):
        lo = ((o % chunks) * seqs + o // chunks) * width
        context_ref[:, lo : lo + width] = values[o]


def sum_kernel(where_ref, *refs, parts, seqs, width):
    outs = refs[parts:]
    for m in range(3):
        sums = []
        for i in range(seqs):
            acc = refs[i][:, m * width : (m + 1) * width].astype(F32)
            for j in range(i + seqs, parts, seqs):
                acc = acc + refs[j][:, m * width : (m + 1) * width].astype(F32)
            sums.append(acc)
        if seqs == 1:
            outs[m][...] = sums[0]
        else:
            flip = where_ref[2] != 0
            outs[m][:, :width] = jnp.where(flip, sums[1], sums[0])
            outs[m][:, width:] = jnp.where(flip, sums[0], sums[1])


def pack_kernel(where_ref, chosen_ref, *refs, lefts, seqs, chunks, width, noted):
    tokens, up = refs[:2]
    weight_refs = refs[2:5]
    hops = len(lefts)
    sends = refs[5 : 5 + hops]
    own_up = refs[5 + hops]
    weight_sends = refs[6 + hops : 6 + hops + seqs]
    sems = refs[6 + hops + seqs]
    model = tokens.shape[1]

    def columns(offset):
        which = (where_ref[0] ^ (offset % chunks)) * seqs + (where_ref[2] ^ (offset // chunks))
        return pl.ds(pl.multiple_of(which * width, width), width)

    copies = []
    for send, left in zip(sends, lefts):
        copies.append((tokens, send.at[:, :model]))
        for k in range(left):
            lo = model + k * width
            copies.append((up.at[:, columns(left + k)], send.at[:, lo : lo + width]))
    copies.append((up.at[:, columns(0)], own_up))
    for i in range(seqs):
        for m in range(3):
            copies.append(
                (
                    weight_refs[m].at[:, columns(i * chunks)],
                    weight_sends[i].at[:, m * width : (m + 1) * width],
                )
            )
    copies = [
        pltpu.make_async_copy(source, target, sems.at[index])
        for index, (source, target) in enumerate(copies)
    ]
    for copy in copies:
        copy.start()
    if noted:
        lo = model + lefts[0] * width
        shape = (tokens.shape[0], 128)
        lane = lax.broadcasted_iota(jnp.int32, shape, 1)
        both = jnp.where(lane < 64, chosen_ref[0], chosen_ref[1])
        sends[0][:, lo : lo + 128] = both.astype(F32).astype(BF16)
    for copy in copies:
        copy.wait()


def per_device(tokens, global_blocks, w_query, w_key, w_value, d_context):
    own_tokens = tokens[0]
    upstream = d_context[0]
    rows, model = own_tokens.shape
    hdim = model // HEADS
    chunks = lax.axis_size("ctx")
    parts = lax.axis_size("dp")
    seqs = 1
    if chunks == 4 and parts % 2 == 0 and model % 1024 == 0 and HEADS % 8 == 0:
        seqs = 2
    groups = chunks * seqs
    width = model // groups
    heads = width // hdim
    position = lax.axis_index("ctx")
    line = lax.axis_index("dp")
    side = line % seqs

    where = jnp.stack([position, line, side]).astype(jnp.int32)
    hops = [("dp", 1, chunks)] if seqs == 2 else []
    bit = chunks // 2
    while bit:
        hops.append(("ctx", bit, bit))
        bit //= 2

    smem = pl.BlockSpec(memory_space=pltpu.SMEM)
    vmem = pl.BlockSpec(memory_space=pltpu.VMEM)
    hbm = pl.BlockSpec(memory_space=pltpu.HBM)
    chosen = global_blocks[0]
    lefts = [groups >> (k + 1) for k in range(len(hops))]
    packed = width % 128 == 0
    noted = 128 if seqs == 2 else 0
    if packed:
        sizes = [model + left * width + (noted if k == 0 else 0) for k, left in enumerate(lefts)]
        outs = pl.pallas_call(
            lambda *refs: pack_kernel(
                *refs, lefts=lefts, seqs=seqs, chunks=chunks, width=width, noted=noted
            ),
            out_shape=tuple(jax.ShapeDtypeStruct((rows, size), BF16) for size in sizes + [width])
            + (jax.ShapeDtypeStruct((model // parts, 3 * width), BF16),) * seqs,
            in_specs=[smem, smem] + [hbm] * 5,
            out_specs=(vmem,) * (len(hops) + 1 + seqs),
            scratch_shapes=[
                pltpu.SemaphoreType.DMA((len(hops) + sum(lefts) + 1 + 3 * seqs,)),
            ],
            compiler_params=pltpu.CompilerParams(vmem_limit_bytes=PACK_VMEM),
            cost_estimate=cost(2),
            name="pack",
        )(where, chosen, own_tokens, upstream, w_query, w_key, w_value)
        own_sends = outs[: len(hops)]
        own_up = outs[len(hops)]
        sends = outs[len(hops) + 1 :]
    else:

        def slice_of(value, offset):
            which = (position ^ (offset % chunks)) * seqs + (side ^ (offset // chunks))
            return lax.dynamic_slice_in_dim(value, which * width, width, 1)

        ups = [slice_of(upstream, o) for o in range(groups)]
        own_up = ups[0]
        own_sends = [
            jnp.concatenate([own_tokens] + ups[left : 2 * left], axis=1) for left in lefts
        ]
        sends = [
            jnp.concatenate(
                [slice_of(w, i * chunks) for w in (w_query, w_key, w_value)], axis=1
            )
            for i in range(seqs)
        ]

    arrived = [xor_permute(own_sends[k], *hops[k][:2]) for k in range(seqs)]
    weights = [sends[0]]
    for j in range(1, parts):
        weights.append(xor_permute(sends[j % seqs], "dp", j))

    length = chunks * rows
    live = global_blocks[0, 0] >= 0

    def guarded(function, *operands):
        return lax.cond(
            live,
            function,
            lambda *values: jax.tree.map(
                lambda v: jnp.zeros(v.shape, v.dtype), jax.eval_shape(function, *values)
            ),
            *operands,
        )

    def attend(buffers, sources, weights, carry=None, carried=(), far_ids=None):
        kind = F32 if carry == "out" else BF16
        results = pl.pallas_call(
            lambda *refs: attention_kernel(
                *refs,
                sources=sources,
                chunks=chunks,
                far_ids=far_ids,
                carry=carry,
                rows=rows,
                heads=heads,
                hdim=hdim,
                parts=parts,
                scale=1.0 / math.sqrt(hdim),
            ),
            out_shape=(jax.ShapeDtypeStruct((model // parts, 3 * width), kind),) * parts
            + (jax.ShapeDtypeStruct((chunks // 2, rows, model + width), BF16),) * 2,
            in_specs=[smem] * 2
            + [pl.BlockSpec(memory_space=pl.ANY)] * (len(buffers) + parts)
            + [vmem] * len(carried),
            out_specs=(vmem,) * (parts + 2),
            scratch_shapes=[
                pltpu.VMEM((length, model), BF16),
                pltpu.VMEM((model, 3 * width), BF16),
                pltpu.VMEM((length, width), BF16),
                pltpu.VMEM((heads, length, 2 * hdim), BF16),
                pltpu.VMEM((heads, 2 * hdim, length), BF16),
                pltpu.VMEM((heads, chunks, 2 * rows, 2 * hdim), BF16),
                pltpu.VMEM((heads, length, 2 * hdim), F32),
                pltpu.VMEM((length, 3 * width), BF16),
                pltpu.VMEM((length, width), BF16),
                pltpu.VMEM((16, 128), BF16),
                pltpu.SemaphoreType.DMA((2 * len(sources) + parts + 1,)),
            ],
            compiler_params=pltpu.CompilerParams(vmem_limit_bytes=24 * 1024 * 1024),
            cost_estimate=cost(14 // seqs),
            name="attention",
        )(where, chosen, *buffers, *weights, *carried)
        return results[:parts], results[parts], results[parts + 1]

    def combine(keep, got):
        count = keep.shape[0]
        return pl.pallas_call(
            lambda *refs: combine_kernel(*refs, model=model),
            out_shape=(jax.ShapeDtypeStruct((rows, model + 2 * width), BF16),) * count,
            in_specs=[vmem] * 2,
            out_specs=(vmem,) * count,
            compiler_params=SMALL,
            cost_estimate=cost(1),
            name="combine",
        )(keep, got)

    def join(mine, theirs):
        return pl.pallas_call(
            lambda *refs: join_kernel(*refs, model=model),
            out_shape=jax.ShapeDtypeStruct((rows, 2 * mine.shape[1] - model), BF16),
            in_specs=[vmem] * 2,
            out_specs=vmem,
            compiler_params=SMALL,
            cost_estimate=cost(1),
            name="join",
        )(mine, theirs)

    def finish(*values):
        return pl.pallas_call(
            lambda *refs: final_kernel(*refs, model=model, seqs=seqs, chunks=chunks),
            out_shape=(jax.ShapeDtypeStruct((rows, model), BF16),) * 2,
            in_specs=[smem] + [vmem] * len(values),
            compiler_params=SMALL,
            cost_estimate=cost(2),
            name="rows_out",
        )(where, *values)

    if seqs == 2:
        line_hop, far_hop, near_hop = [hop[:2] for hop in hops]
        tz, tx = arrived

        def share(own, tx):
            rest = jnp.concatenate([tx[:, :model], tx[:, model + width :]], axis=1)
            return xor_permute(jnp.concatenate([own, rest], axis=0), *near_hop)

        shared = guarded(share, own_sends[2], tx)

        def both(tz, tx, shared, own_tokens, own_up, *weights):
            lo = model + 2 * width
            part = rows // 2
            txz = [
                xor_permute(
                    jnp.concatenate([piece[:, :model], piece[:, lo : lo + 2 * width]], axis=1),
                    *far_hop,
                )
                for piece in (tz[:part], tz[part:])
            ]
            first, keep, send = attend(
                (own_tokens, shared, tx, own_up),
                (
                    (0, 0, rows, 3, 0),
                    (1, 0, rows, 1, model),
                    (2, 0, rows, 2, model),
                    (1, rows, rows, 1, model),
                ),
                weights,
                carry="out",
            )
            first = list(first)
            txz, first[0] = lax.optimization_barrier((txz, first[0]))
            ctz = xor_permute(tz, *near_hop)
            ctxz = [xor_permute(piece, *near_hop) for piece in txz]
            up = model + width
            grad_w, keep_other, send_other = attend(
                (tz, ctz, *txz, *ctxz),
                (
                    (0, 0, rows, 0, model),
                    (1, 0, rows, 1, up),
                    (2, 0, part, 2, model),
                    (3, 0, part, 3, model),
                    (4, 0, part, 4, up),
                    (5, 0, part, 5, up),
                ),
                weights,
                carry="in",
                carried=first,
                far_ids=model + 4 * width,
            )
            return grad_w, keep, send, keep_other, send_other

        grad_w, *rest = both(tz, tx, shared, own_tokens, own_up, *weights)

        def collect(keep, send, keep_other, send_other):
            held, far = combine(keep_other, xor_permute(send_other, *near_hop))
            mine, near = combine(keep, xor_permute(send, *near_hop))
            held = join(held, xor_permute(far, *far_hop))
            far = xor_permute(held, *line_hop)
            return finish(mine, xor_permute(near, *far_hop), far)

        moved = [grad_w[0]] + [xor_permute(grad_w[j], "dp", j) for j in range(1, parts)]
        grad_tokens, context = guarded(collect, *rest)
    else:

        def spread(first, *own):
            pieces = {hops[0][2]: first}
            for k in range(1, len(hops)):
                axis, bit, offset = hops[k]
                lo = model + lefts[k] * width
                for key in list(pieces):
                    value = pieces[key]
                    value = jnp.concatenate(
                        [value[:, :model], value[:, lo : lo + lefts[k] * width]], axis=1
                    )
                    pieces[key + offset] = xor_permute(value, axis, bit)
                pieces[offset] = xor_permute(own[k - 1], axis, bit)
            return tuple(pieces[o] for o in range(1, groups))

        pieces = guarded(spread, arrived[0], *own_sends[1:])
        ups = [own_up] + [value[:, model : model + width] for value in pieces]
        buffers = [own_tokens] + [value[:, :model] for value in pieces] + ups
        grad_w, keep, send = attend(
            buffers, [(o, 0, rows, groups + o, 0) for o in range(groups)], weights
        )

        def collect(keep, send):
            held = combine(keep, xor_permute(send, *hops[-1][:2]))
            for axis, bit, _ in reversed(hops[1:-1]):
                theirs = [xor_permute(value, axis, bit) for value in held[1::2]]
                held = [join(*pair) for pair in zip(held[::2], theirs)]
            return finish(held[0], xor_permute(held[1], *hops[0][:2]))

        moved = [grad_w[0]] + [xor_permute(grad_w[j], "dp", j) for j in range(1, parts)]
        grad_tokens, context = guarded(collect, keep, send)

    final = pl.pallas_call(
        lambda *refs: sum_kernel(*refs, parts=parts, seqs=seqs, width=width),
        out_shape=(jax.ShapeDtypeStruct((model // parts, seqs * width), F32),) * 3,
        in_specs=[smem] + [vmem] * parts,
        compiler_params=SMALL,
        cost_estimate=cost(2),
        name="weights_out",
    )(where, *moved)
    return (context[None], grad_tokens[None], *final)


def solution(mesh):
    return jax.shard_map(
        per_device,
        mesh=mesh,
        in_specs=(
            P(("groups", "dp"), "ctx", None),
            P(("groups", "dp"), None),
            P("dp", None),
            P("dp", None),
            P("dp", None),
            P(("groups", "dp"), "ctx", None),
        ),
        out_specs=(
            P(("groups", "dp"), "ctx", None),
            P(("groups", "dp"), "ctx", None),
            P(("groups", "dp"), "ctx"),
            P(("groups", "dp"), "ctx"),
            P(("groups", "dp"), "ctx"),
        ),
        check_vma=False,
    )
```

```python
import math

import jax
import jax.numpy as jnp
from jax import lax
from jax.experimental import pallas as pl
from jax.experimental.pallas import tpu as pltpu
from jax.sharding import PartitionSpec as P

HEADS = 16
BLK = 64
NEG = -1e30
SPAN = 4

NT = (((1,), (1,)), ((), ()))
TN = (((0,), (0,)), ((), ()))
F32 = jnp.float32
BF16 = jnp.bfloat16


SMALL = pltpu.CompilerParams(vmem_limit_bytes=8 * 1024 * 1024)


def cost(micros):
    return pl.CostEstimate(
        flops=0, transcendentals=0, bytes_accessed=int(micros * 3_000_000)
    )


def xor_permute(value, axis, bit):
    count = lax.axis_size(axis)
    return lax.ppermute(value, axis, [(i, i ^ bit) for i in range(count)])


def attention_kernel(
    where_ref, chosen_ref, *refs, sources, chunks, far_ids, carry, rows, heads, hdim, parts, scale
):
    half = chunks // 2
    count = 1 + max(max(source[0], source[3]) for source in sources)
    buffers = refs[:count]
    weight_refs = refs[count : count + parts]
    carried = refs[count + parts : count + 2 * parts] if carry == "in" else None
    outs = refs[count + (2 if carry == "in" else 1) * parts :]
    grad_w_refs = outs[:parts]
    keep_ref, send_ref = outs[parts : parts + 2]
    (
        all_tokens, weight, up_all, kv_s, kvt_s, pair_s, dkv_s, grads, context_s, noted, sems
    ) = outs[parts + 2 :]
    length = chunks * rows
    width = heads * hdim
    model = all_tokens.shape[1]
    part_rows = model // parts
    position = where_ref[0]
    line = where_ref[1]

    copies = []
    for j in range(parts):
        start = pl.multiple_of((line ^ j) * part_rows, part_rows)
        copies.append((weight_refs[j], weight.at[pl.ds(start, part_rows), :]))
    at = 0
    for index, first, size, up, start in sources:
        target = pl.ds(at, size)
        held = pl.ds(first, size)
        copies.append((buffers[index].at[held, :model], all_tokens.at[target, :]))
        if up != index:
            held = pl.ds(0, size)
        copies.append((buffers[up].at[held, start : start + width], up_all.at[target, :]))
        at += size
    if far_ids is not None:
        copies.append((buffers[0].at[:16, far_ids : far_ids + 128], noted))
    copies = [
        pltpu.make_async_copy(source, target, sems.at[index])
        for index, (source, target) in enumerate(copies)
    ]
    for copy in copies:
        copy.start()
    pair_s[...] = jnp.zeros_like(pair_s)
    if SPAN < chunks:
        dkv_s[...] = jnp.zeros_like(dkv_s)
    for copy in copies:
        copy.wait()
    if far_ids is None:
        chosen = [chosen_ref[k] for k in range(2)]
    else:
        chosen = [noted[:1, 64 * k : 64 * k + 1].astype(F32).astype(jnp.int32) for k in range(2)]
        chosen = [jnp.broadcast_to(value, (1, rows)) for value in chosen]

    tile = min(512, length)

    @pl.loop(0, length // tile)
    def _(t):
        at = pl.ds(pl.multiple_of(t * tile, tile), tile)
        out = jnp.dot(all_tokens[at, :], weight[...], preferred_element_type=F32)
        for h in range(heads):
            lo = h * hdim
            kv = jnp.concatenate(
                [
                    out[:, width + lo : width + lo + hdim],
                    out[:, 2 * width + lo : 2 * width + lo + hdim],
                ],
                axis=1,
            )
            kv_s[h, at, :] = kv.astype(BF16)
            kvt_s[h, :, at] = jnp.transpose(kv).astype(BF16)
            q = (out[:, lo : lo + hdim].astype(BF16) * scale).astype(BF16)
            for p in range(tile // rows):
                pair_s[h, t * (tile // rows) + p, :rows, :hdim] = q[p * rows : (p + 1) * rows]
    for h in range(heads):
        for b in range(chunks):
            pair_s[h, b, rows:, hdim:] = up_all[
                b * rows : (b + 1) * rows, h * hdim : (h + 1) * hdim
            ]

    blocks_per_chunk = rows // BLK
    block_count = length // BLK
    log_blocks = int(math.log2(blocks_per_chunk))

    span = min(SPAN, chunks)

    @pl.loop(0, chunks // span)
    def _(t):
        first, second = chosen
        shape = (block_count, 1, rows)
        key = lax.broadcasted_iota(jnp.int32, shape, 0)
        key_block = (lax.shift_right_logical(key, log_blocks) ^ position) * blocks_per_chunk + (
            key & (blocks_per_chunk - 1)
        )
        offset = lax.shift_right_logical(
            lax.broadcasted_iota(jnp.int32, shape, 2), int(math.log2(BLK))
        )
        biases = []
        for p in range(span):
            j = t * span + p
            query_block = (position ^ j) * blocks_per_chunk + offset
            keep = (
                (jnp.abs(key_block - query_block) <= 1)
                | (key_block == first)
                | (key_block == second)
                | (query_block == first)
                | (query_block == second)
            )
            biases.append(jnp.where(keep, 0.0, NEG))
        for h in range(heads):
            pair = pair_s[h, pl.ds(t * span, span)].reshape(span * 2 * rows, 2 * hdim)
            both = lax.dot_general(kv_s[h], pair, NT, preferred_element_type=F32)
            parts_of = [both[:, p * rows : (p + 1) * rows] for p in range(2 * span)]
            forward = []
            backward = []
            inverses = []
            for p in range(span):
                scores = parts_of[2 * p].reshape(block_count, BLK, rows) + biases[p]
                scores = scores.reshape(length, rows)
                grad_probs = parts_of[2 * p + 1]
                raw = jnp.exp(scores - jnp.max(scores, axis=0, keepdims=True))
                inverse = 1.0 / jnp.sum(raw, axis=0, keepdims=True)
                raw_low = raw.astype(BF16)
                probs = raw * inverse
                delta = inverse * jnp.sum(
                    raw_low.astype(F32) * grad_probs, axis=0, keepdims=True
                )
                low = (probs * (grad_probs - delta)).astype(BF16)
                forward += [raw_low, low]
                backward += [low, probs.astype(BF16)]
                inverses.append(inverse)
            sums = jnp.dot(
                kvt_s[h],
                jnp.concatenate(forward, axis=1),
                preferred_element_type=F32,
            )
            dkv = jnp.dot(
                jnp.concatenate(backward, axis=1), pair, preferred_element_type=F32
            )
            if span == chunks:
                dkv_s[h] = dkv
            else:
                dkv_s[h] += dkv
            lo = h * hdim
            for p in range(span):
                at = pl.ds(pl.multiple_of((t * span + p) * rows, rows), rows)
                lanes = 2 * p * rows
                rows_out = jnp.transpose(
                    jnp.concatenate(
                        [
                            sums[:hdim, lanes + rows : lanes + 2 * rows] * scale,
                            sums[hdim:, lanes : lanes + rows] * inverses[p],
                        ],
                        axis=0,
                    )
                ).astype(BF16)
                grads[at, lo : lo + hdim] = rows_out[:, :hdim]
                context_s[at, lo : lo + hdim] = rows_out[:, hdim:]

    for h in range(heads):
        lo = h * hdim
        grads[:, width + lo : width + lo + hdim] = dkv_s[h, :, :hdim].astype(BF16)
        grads[:, 2 * width + lo : 2 * width + lo + hdim] = dkv_s[h, :, hdim:].astype(BF16)

    for j in range(parts):
        cols = pl.ds(pl.multiple_of((line ^ j) * part_rows, part_rows), part_rows)
        out = lax.dot_general(all_tokens[:, cols], grads[...], TN, preferred_element_type=F32)
        if carry == "in":
            out = out + carried[j][...]
        grad_w_refs[j][...] = out.astype(grad_w_refs[j].dtype)

    @pl.loop(0, half)
    def _(t):
        at = pl.ds(pl.multiple_of(t * 2 * rows, 2 * rows), 2 * rows)
        out = lax.dot_general(grads[at, :], weight[...], NT, preferred_element_type=F32)
        keep_ref[t, :, :model] = out[:rows].astype(BF16)
        send_ref[t, :, :model] = out[rows:].astype(BF16)
        keep_ref[t, :, model:] = context_s[pl.ds(pl.multiple_of(t * 2 * rows, rows), rows), :]
        send_ref[t, :, model:] = context_s[
            pl.ds(pl.multiple_of(t * 2 * rows + rows, rows), rows), :
        ]


def add_and_join(mine, theirs, model):
    total = (mine[:, :model].astype(F32) + theirs[:, :model].astype(F32)).astype(BF16)
    return [total, mine[:, model:], theirs[:, model:]]


def put(out_ref, first, values):
    size = values[0].shape[0]
    lo = 0
    for value in values:
        out_ref[first : first + size, lo : lo + value.shape[1]] = value
        lo += value.shape[1]


def combine_kernel(keep_ref, got_ref, *outs, model):
    for t in range(keep_ref.shape[0]):
        put(outs[t], 0, add_and_join(keep_ref[t], got_ref[t], model))


def join_kernel(mine_ref, theirs_ref, out_ref, *, model):
    put(out_ref, 0, add_and_join(mine_ref[...], theirs_ref[...], model))


def final_kernel(where_ref, *refs, model, seqs, chunks, parts):
    outs = refs[-5:]
    grad_ref, context_ref = outs[:2]
    ins = refs[: -5 - parts]
    moved = refs[-5 - parts : -5]
    if len(ins) == 2:
        total = ins[0][:, :model]
        mine = ins[0][:, model:]
        far = ins[1][...]
    else:
        total, mine, near = add_and_join(ins[0][...], ins[1][...], model)
        mine = jnp.concatenate([mine, near], axis=1)
        far = ins[2][...]
    grad_ref[...] = (total.astype(F32) + far[:, :model].astype(F32)).astype(BF16)
    theirs = far[:, model:]
    groups = seqs * chunks
    width = model // groups
    values = [mine[:, k * width : (k + 1) * width] for k in range(groups // 2)]
    values += [theirs[:, k * width : (k + 1) * width] for k in range(groups // 2)]
    own = where_ref[0] + where_ref[2] * chunks
    bit = 1
    while bit < groups:
        flip = (own & bit) != 0
        values = [jnp.where(flip, values[o ^ bit], values[o]) for o in range(groups)]
        bit *= 2
    for o in range(groups):
        lo = ((o % chunks) * seqs + o // chunks) * width
        context_ref[:, lo : lo + width] = values[o]
    for m in range(3):
        sums = []
        for i in range(seqs):
            acc = moved[i][:, m * width : (m + 1) * width].astype(F32)
            for j in range(i + seqs, parts, seqs):
                acc = acc + moved[j][:, m * width : (m + 1) * width].astype(F32)
            sums.append(acc)
        if seqs == 1:
            outs[2 + m][...] = sums[0]
        else:
            flip = where_ref[2] != 0
            outs[2 + m][:, :width] = jnp.where(flip, sums[1], sums[0])
            outs[2 + m][:, width:] = jnp.where(flip, sums[0], sums[1])


def pack_kernel(where_ref, blocks_ref, *refs, lefts, seqs, chunks, width, noted):
    tokens, up = refs[:2]
    weight_refs = refs[2:5]
    hops = len(lefts)
    sends = refs[5 : 5 + hops]
    own_up = refs[5 + hops]
    weight_sends = refs[6 + hops : 6 + hops + seqs]
    note, blocks, sems = refs[6 + hops + seqs :]
    fetch = pltpu.make_async_copy(blocks_ref, blocks, sems.at[sems.shape[0] - 1])
    fetch.start()
    model = tokens.shape[1]

    def columns(offset):
        which = (where_ref[0] ^ (offset % chunks)) * seqs + (where_ref[2] ^ (offset // chunks))
        return pl.ds(pl.multiple_of(which * width, width), width)

    copies = []
    for send, left in zip(sends, lefts):
        copies.append((tokens, send.at[:, :model]))
        for k in range(left):
            lo = model + k * width
            copies.append((up.at[:, columns(left + k)], send.at[:, lo : lo + width]))
    copies.append((up.at[:, columns(0)], own_up))
    for i in range(seqs):
        for m in range(3):
            copies.append(
                (
                    weight_refs[m].at[:, columns(i * chunks)],
                    weight_sends[i].at[:, m * width : (m + 1) * width],
                )
            )
    copies = [
        pltpu.make_async_copy(source, target, sems.at[index])
        for index, (source, target) in enumerate(copies)
    ]
    for copy in copies:
        copy.start()
    fetch.wait()
    if noted:
        lane = lax.broadcasted_iota(jnp.int32, note.shape, 1)
        note[...] = jnp.where(lane < 64, blocks[0, 0], blocks[0, 1]).astype(F32).astype(BF16)
        lo = model + lefts[0] * width
        sends[0][:, lo : lo + 128] = note[...]
    for copy in copies:
        copy.wait()


def per_device(tokens, global_blocks, w_query, w_key, w_value, d_context):
    own_tokens = tokens[0]
    upstream = d_context[0]
    rows, model = own_tokens.shape
    hdim = model // HEADS
    chunks = lax.axis_size("ctx")
    parts = lax.axis_size("dp")
    seqs = 1
    if chunks == 4 and parts % 2 == 0 and model % 1024 == 0 and HEADS % 8 == 0 and rows % 32 == 0:
        seqs = 2
    groups = chunks * seqs
    width = model // groups
    heads = width // hdim
    position = lax.axis_index("ctx")
    line = lax.axis_index("dp")
    side = line % seqs

    where = jnp.stack([position, line, side]).astype(jnp.int32)
    hops = [("dp", 1, chunks)] if seqs == 2 else []
    bit = chunks // 2
    while bit:
        hops.append(("ctx", bit, bit))
        bit //= 2

    smem = pl.BlockSpec(memory_space=pltpu.SMEM)
    vmem = pl.BlockSpec(memory_space=pltpu.VMEM)
    hbm = pl.BlockSpec(memory_space=pltpu.HBM)
    chosen = global_blocks[0]
    lefts = [groups >> (k + 1) for k in range(len(hops))]
    packed = width % 128 == 0
    noted = 128 if seqs == 2 else 0
    if packed:
        sizes = [model + left * width + (noted if k == 0 else 0) for k, left in enumerate(lefts)]
        outs = pl.pallas_call(
            lambda *refs: pack_kernel(
                *refs, lefts=lefts, seqs=seqs, chunks=chunks, width=width, noted=noted
            ),
            out_shape=tuple(jax.ShapeDtypeStruct((rows, size), BF16) for size in sizes + [width])
            + (jax.ShapeDtypeStruct((model // parts, 3 * width), BF16),) * seqs,
            in_specs=[smem] + [hbm] * 6,
            out_specs=(vmem,) * (len(hops) + 1 + seqs),
            scratch_shapes=[
                pltpu.VMEM((rows, 128), BF16),
                pltpu.SMEM((1, 2), jnp.int32),
                pltpu.SemaphoreType.DMA((len(hops) + sum(lefts) + 2 + 3 * seqs,)),
            ],
            compiler_params=SMALL,
            cost_estimate=cost(2),
            name="pack",
        )(
            where,
            *[
                pltpu.with_memory_space_constraint(value, pltpu.HBM)
                for value in (global_blocks, own_tokens, upstream, w_query, w_key, w_value)
            ],
        )
        own_sends = outs[: len(hops)]
        own_up = outs[len(hops)]
        sends = outs[len(hops) + 1 :]
    else:

        def slice_of(value, offset):
            which = (position ^ (offset % chunks)) * seqs + (side ^ (offset // chunks))
            return lax.dynamic_slice_in_dim(value, which * width, width, 1)

        ups = [slice_of(upstream, o) for o in range(groups)]
        own_up = ups[0]
        own_sends = [
            jnp.concatenate([own_tokens] + ups[left : 2 * left], axis=1) for left in lefts
        ]
        sends = [
            jnp.concatenate(
                [slice_of(w, i * chunks) for w in (w_query, w_key, w_value)], axis=1
            )
            for i in range(seqs)
        ]

    arrived = [xor_permute(own_sends[k], *hops[k][:2]) for k in range(seqs)]
    weights = [sends[0]]
    for j in range(1, parts):
        weights.append(xor_permute(sends[j % seqs], "dp", j))

    length = chunks * rows
    live = global_blocks[0, 0] >= 0

    def guarded(function, *operands):
        return lax.cond(
            live,
            function,
            lambda *values: jax.tree.map(
                lambda v: jnp.zeros(v.shape, v.dtype), jax.eval_shape(function, *values)
            ),
            *operands,
        )

    def attend(buffers, sources, weights, carry=None, carried=(), far_ids=None):
        kind = F32 if carry == "out" else BF16
        results = pl.pallas_call(
            lambda *refs: attention_kernel(
                *refs,
                sources=sources,
                chunks=chunks,
                far_ids=far_ids,
                carry=carry,
                rows=rows,
                heads=heads,
                hdim=hdim,
                parts=parts,
                scale=1.0 / math.sqrt(hdim),
            ),
            out_shape=(jax.ShapeDtypeStruct((model // parts, 3 * width), kind),) * parts
            + (jax.ShapeDtypeStruct((chunks // 2, rows, model + width), BF16),) * 2,
            in_specs=[smem] * 2
            + [pl.BlockSpec(memory_space=pl.ANY)] * (len(buffers) + parts)
            + [vmem] * len(carried),
            out_specs=(vmem,) * (parts + 2),
            scratch_shapes=[
                pltpu.VMEM((length, model), BF16),
                pltpu.VMEM((model, 3 * width), BF16),
                pltpu.VMEM((length, width), BF16),
                pltpu.VMEM((heads, length, 2 * hdim), BF16),
                pltpu.VMEM((heads, 2 * hdim, length), BF16),
                pltpu.VMEM((heads, chunks, 2 * rows, 2 * hdim), BF16),
                pltpu.VMEM((heads, length, 2 * hdim), F32),
                pltpu.VMEM((length, 3 * width), BF16),
                pltpu.VMEM((length, width), BF16),
                pltpu.VMEM((16, 128), BF16),
                pltpu.SemaphoreType.DMA((2 * len(sources) + parts + 1,)),
            ],
            compiler_params=pltpu.CompilerParams(vmem_limit_bytes=24 * 1024 * 1024),
            cost_estimate=cost(14 // seqs),
            name="attention",
        )(where, chosen, *buffers, *weights, *carried)
        return results[:parts], results[parts], results[parts + 1]

    def combine(keep, got):
        kinds = (jax.ShapeDtypeStruct((rows, model + 2 * width), BF16),) * keep.shape[0]
        return pl.pallas_call(
            lambda *refs: combine_kernel(*refs, model=model),
            out_shape=kinds,
            in_specs=[vmem] * 2,
            out_specs=(vmem,) * len(kinds),
            compiler_params=SMALL,
            cost_estimate=cost(1),
            name="combine",
        )(keep, got)

    def join(mine, theirs):
        return pl.pallas_call(
            lambda *refs: join_kernel(*refs, model=model),
            out_shape=jax.ShapeDtypeStruct((mine.shape[0], 2 * mine.shape[1] - model), BF16),
            in_specs=[vmem] * 2,
            out_specs=vmem,
            compiler_params=SMALL,
            cost_estimate=cost(1),
            name="join",
        )(mine, theirs)

    if seqs == 2:
        line_hop, far_hop, near_hop = [hop[:2] for hop in hops]
        tz, tx = arrived

        def share(own, tx):
            rest = jnp.concatenate([tx[:, :model], tx[:, model + width :]], axis=1)
            return xor_permute(jnp.concatenate([own, rest], axis=0), *near_hop)

        shared = guarded(share, own_sends[2], tx)

        def both(tz, tx, shared, own_tokens, own_up, *weights):
            lo = model + 2 * width
            part = rows // 2
            txz = [
                xor_permute(
                    jnp.concatenate([piece[:, :model], piece[:, lo : lo + 2 * width]], axis=1),
                    *far_hop,
                )
                for piece in (tz[:part], tz[part:])
            ]
            first, keep, send = attend(
                (own_tokens, shared, tx, own_up),
                (
                    (0, 0, rows, 3, 0),
                    (1, 0, rows, 1, model),
                    (2, 0, rows, 2, model),
                    (1, rows, rows, 1, model),
                ),
                weights,
                carry="out",
            )
            first = list(first)
            txz, first[0] = lax.optimization_barrier((txz, first[0]))
            ctz = xor_permute(tz, *near_hop)
            ctxz = [xor_permute(piece, *near_hop) for piece in txz]
            up = model + width
            grad_w, keep_other, send_other = attend(
                (tz, ctz, *txz, *ctxz),
                (
                    (0, 0, rows, 0, model),
                    (1, 0, rows, 1, up),
                    (2, 0, part, 2, model),
                    (3, 0, part, 3, model),
                    (4, 0, part, 4, up),
                    (5, 0, part, 5, up),
                ),
                weights,
                carry="in",
                carried=first,
                far_ids=model + 4 * width,
            )
            return grad_w, keep, send, keep_other, send_other

        grad_w, *rest = both(tz, tx, shared, own_tokens, own_up, *weights)

        keep, send, keep_other, send_other = rest
        got_other = xor_permute(send_other, *near_hop)
        got = xor_permute(send, *near_hop)
        moved = [grad_w[0]] + [xor_permute(grad_w[j], "dp", j) for j in range(1, parts)]

        def collect(keep, got, keep_other, got_other):
            held, far = combine(keep_other, got_other)
            far = xor_permute(join(held, xor_permute(far, *far_hop)), *line_hop)
            mine, near = combine(keep, got)
            return mine, xor_permute(near, *far_hop), far

        ins = guarded(collect, keep, got, keep_other, got_other)
    else:

        def spread(first, *own):
            pieces = {hops[0][2]: first}
            for k in range(1, len(hops)):
                axis, bit, offset = hops[k]
                lo = model + lefts[k] * width
                for key in list(pieces):
                    value = pieces[key]
                    value = jnp.concatenate(
                        [value[:, :model], value[:, lo : lo + lefts[k] * width]], axis=1
                    )
                    pieces[key + offset] = xor_permute(value, axis, bit)
                pieces[offset] = xor_permute(own[k - 1], axis, bit)
            return tuple(pieces[o] for o in range(1, groups))

        pieces = guarded(spread, arrived[0], *own_sends[1:])
        ups = [own_up] + [value[:, model : model + width] for value in pieces]
        buffers = [own_tokens] + [value[:, :model] for value in pieces] + ups
        grad_w, keep, send = attend(
            buffers, [(o, 0, rows, groups + o, 0) for o in range(groups)], weights
        )

        def collect(keep, send):
            held = combine(keep, xor_permute(send, *hops[-1][:2]))
            for axis, bit, _ in reversed(hops[1:-1]):
                theirs = [xor_permute(value, axis, bit) for value in held[1::2]]
                held = [join(*pair) for pair in zip(held[::2], theirs)]
            return held[0], xor_permute(held[1], *hops[0][:2])

        moved = [grad_w[0]] + [xor_permute(grad_w[j], "dp", j) for j in range(1, parts)]
        ins = guarded(collect, keep, send)

    grad_tokens, context, *final = pl.pallas_call(
        lambda *refs: final_kernel(*refs, model=model, seqs=seqs, chunks=chunks, parts=parts),
        out_shape=(jax.ShapeDtypeStruct((rows, model), BF16),) * 2
        + (jax.ShapeDtypeStruct((model // parts, seqs * width), F32),) * 3,
        in_specs=[smem] + [vmem] * (len(ins) + len(moved)),
        compiler_params=SMALL,
        cost_estimate=cost(2),
        name="finish",
    )(where, *ins, *moved)
    return (context[None], grad_tokens[None], *final)


def solution(mesh):
    return jax.shard_map(
        per_device,
        mesh=mesh,
        in_specs=(
            P(("groups", "dp"), "ctx", None),
            P(("groups", "dp"), None),
            P("dp", None),
            P("dp", None),
            P("dp", None),
            P(("groups", "dp"), "ctx", None),
        ),
        out_specs=(
            P(("groups", "dp"), "ctx", None),
            P(("groups", "dp"), "ctx", None),
            P(("groups", "dp"), "ctx"),
            P(("groups", "dp"), "ctx"),
            P(("groups", "dp"), "ctx"),
        ),
        check_vma=False,
    )
```

```python
import math

import jax
import jax.numpy as jnp
from jax import lax
from jax.experimental import pallas as pl
from jax.experimental.pallas import tpu as pltpu
from jax.sharding import PartitionSpec as P

HEADS = 16
BLK = 64
NEG = -1e30
SPAN = 4

NT = (((1,), (1,)), ((), ()))
TN = (((0,), (0,)), ((), ()))
F32 = jnp.float32
BF16 = jnp.bfloat16


SMALL = pltpu.CompilerParams(vmem_limit_bytes=8 * 1024 * 1024)


def cost(micros):
    return pl.CostEstimate(
        flops=0, transcendentals=0, bytes_accessed=int(micros * 3_000_000)
    )


def xor_permute(value, axis, bit):
    count = lax.axis_size(axis)
    return lax.ppermute(value, axis, [(i, i ^ bit) for i in range(count)])


def attention_kernel(
    where_ref, chosen_ref, *refs, sources, shares, chunks, far_ids, carry, rows, heads, hdim, parts, scale
):
    half = chunks // 2
    count = 1 + max(max(source[0], source[3]) for source in sources)
    buffers = refs[:count]
    weight_refs = refs[count : count + len(shares)]
    refs = refs[count + len(shares) :]
    carried = refs[:parts] if carry == "in" else None
    outs = refs[parts:] if carry == "in" else refs
    grad_w_refs = outs[:parts]
    keep_ref, send_ref = outs[parts : parts + 2]
    (
        all_tokens, weight, up_all, kv_s, kvt_s, pair_s, dkv_s, grads, context_s, noted, sems
    ) = outs[parts + 2 :]
    length = chunks * rows
    width = heads * hdim
    model = all_tokens.shape[1]
    part_rows = model // parts
    position = where_ref[0]
    line = where_ref[1]

    copies = []
    for ref, (j, side) in zip(weight_refs, shares):
        size = ref.shape[0]
        start = (line ^ j) * part_rows
        if side is not None:
            start = start + (where_ref[3] ^ side) * size
        target = pl.ds(pl.multiple_of(start, size), size)
        copies.append((ref, weight.at[target, :]))
    at = 0
    for index, first, size, up, start in sources:
        target = pl.ds(at, size)
        held = pl.ds(first, size)
        copies.append((buffers[index].at[held, :model], all_tokens.at[target, :]))
        if up != index:
            held = pl.ds(0, size)
        copies.append((buffers[up].at[held, start : start + width], up_all.at[target, :]))
        at += size
    if far_ids is not None:
        copies.append((buffers[0].at[:16, far_ids : far_ids + 128], noted))
    copies = [
        pltpu.make_async_copy(source, target, sems.at[index])
        for index, (source, target) in enumerate(copies)
    ]
    for copy in copies:
        copy.start()
    pair_s[...] = jnp.zeros_like(pair_s)
    if SPAN < chunks:
        dkv_s[...] = jnp.zeros_like(dkv_s)
    for copy in copies:
        copy.wait()
    if far_ids is None:
        chosen = [chosen_ref[k] for k in range(2)]
    else:
        chosen = [noted[:1, 64 * k : 64 * k + 1].astype(F32).astype(jnp.int32) for k in range(2)]
        chosen = [jnp.broadcast_to(value, (1, rows)) for value in chosen]

    tile = min(512, length)

    @pl.loop(0, length // tile)
    def _(t):
        at = pl.ds(pl.multiple_of(t * tile, tile), tile)
        out = jnp.dot(all_tokens[at, :], weight[...], preferred_element_type=F32)
        for h in range(heads):
            lo = h * hdim
            kv = jnp.concatenate(
                [
                    out[:, width + lo : width + lo + hdim],
                    out[:, 2 * width + lo : 2 * width + lo + hdim],
                ],
                axis=1,
            )
            kv_s[h, at, :] = kv.astype(BF16)
            kvt_s[h, :, at] = jnp.transpose(kv).astype(BF16)
            q = (out[:, lo : lo + hdim].astype(BF16) * scale).astype(BF16)
            for p in range(tile // rows):
                pair_s[h, t * (tile // rows) + p, :rows, :hdim] = q[p * rows : (p + 1) * rows]
    for h in range(heads):
        for b in range(chunks):
            pair_s[h, b, rows:, hdim:] = up_all[
                b * rows : (b + 1) * rows, h * hdim : (h + 1) * hdim
            ]

    blocks_per_chunk = rows // BLK
    block_count = length // BLK
    log_blocks = int(math.log2(blocks_per_chunk))

    span = min(SPAN, chunks)

    @pl.loop(0, chunks // span)
    def _(t):
        first, second = chosen
        shape = (block_count, 1, rows)
        key = lax.broadcasted_iota(jnp.int32, shape, 0)
        key_block = (lax.shift_right_logical(key, log_blocks) ^ position) * blocks_per_chunk + (
            key & (blocks_per_chunk - 1)
        )
        offset = lax.shift_right_logical(
            lax.broadcasted_iota(jnp.int32, shape, 2), int(math.log2(BLK))
        )
        biases = []
        for p in range(span):
            j = t * span + p
            query_block = (position ^ j) * blocks_per_chunk + offset
            keep = (
                (jnp.abs(key_block - query_block) <= 1)
                | (key_block == first)
                | (key_block == second)
                | (query_block == first)
                | (query_block == second)
            )
            biases.append(jnp.where(keep, 0.0, NEG))
        for h in range(heads):
            pair = pair_s[h, pl.ds(t * span, span)].reshape(span * 2 * rows, 2 * hdim)
            both = lax.dot_general(kv_s[h], pair, NT, preferred_element_type=F32)
            parts_of = [both[:, p * rows : (p + 1) * rows] for p in range(2 * span)]
            forward = []
            backward = []
            inverses = []
            for p in range(span):
                scores = parts_of[2 * p].reshape(block_count, BLK, rows) + biases[p]
                scores = scores.reshape(length, rows)
                grad_probs = parts_of[2 * p + 1]
                raw = jnp.exp(scores - jnp.max(scores, axis=0, keepdims=True))
                inverse = 1.0 / jnp.sum(raw, axis=0, keepdims=True)
                raw_low = raw.astype(BF16)
                probs = raw * inverse
                delta = inverse * jnp.sum(
                    raw_low.astype(F32) * grad_probs, axis=0, keepdims=True
                )
                low = (probs * (grad_probs - delta)).astype(BF16)
                forward += [raw_low, low]
                backward += [low, probs.astype(BF16)]
                inverses.append(inverse)
            sums = jnp.dot(
                kvt_s[h],
                jnp.concatenate(forward, axis=1),
                preferred_element_type=F32,
            )
            dkv = jnp.dot(
                jnp.concatenate(backward, axis=1), pair, preferred_element_type=F32
            )
            if span == chunks:
                dkv_s[h] = dkv
            else:
                dkv_s[h] += dkv
            lo = h * hdim
            for p in range(span):
                at = pl.ds(pl.multiple_of((t * span + p) * rows, rows), rows)
                lanes = 2 * p * rows
                rows_out = jnp.transpose(
                    jnp.concatenate(
                        [
                            sums[:hdim, lanes + rows : lanes + 2 * rows] * scale,
                            sums[hdim:, lanes : lanes + rows] * inverses[p],
                        ],
                        axis=0,
                    )
                ).astype(BF16)
                grads[at, lo : lo + hdim] = rows_out[:, :hdim]
                context_s[at, lo : lo + hdim] = rows_out[:, hdim:]

    for h in range(heads):
        lo = h * hdim
        grads[:, width + lo : width + lo + hdim] = dkv_s[h, :, :hdim].astype(BF16)
        grads[:, 2 * width + lo : 2 * width + lo + hdim] = dkv_s[h, :, hdim:].astype(BF16)

    for j in range(parts):
        cols = pl.ds(pl.multiple_of((line ^ j) * part_rows, part_rows), part_rows)
        out = lax.dot_general(all_tokens[:, cols], grads[...], TN, preferred_element_type=F32)
        if carry == "in":
            out = out + carried[j][...]
        grad_w_refs[j][...] = out.astype(grad_w_refs[j].dtype)

    @pl.loop(0, half)
    def _(t):
        at = pl.ds(pl.multiple_of(t * 2 * rows, 2 * rows), 2 * rows)
        out = lax.dot_general(grads[at, :], weight[...], NT, preferred_element_type=F32)
        keep_ref[t, :, :model] = out[:rows].astype(BF16)
        send_ref[t, :, :model] = out[rows:].astype(BF16)
        keep_ref[t, :, model:] = context_s[pl.ds(pl.multiple_of(t * 2 * rows, rows), rows), :]
        send_ref[t, :, model:] = context_s[
            pl.ds(pl.multiple_of(t * 2 * rows + rows, rows), rows), :
        ]


def add_and_join(mine, theirs, model):
    total = (mine[:, :model].astype(F32) + theirs[:, :model].astype(F32)).astype(BF16)
    return [total, mine[:, model:], theirs[:, model:]]


def put(out_ref, first, values):
    size = values[0].shape[0]
    lo = 0
    for value in values:
        out_ref[first : first + size, lo : lo + value.shape[1]] = value
        lo += value.shape[1]


def combine_kernel(keep_ref, got_ref, *outs, model):
    for t in range(keep_ref.shape[0]):
        put(outs[t], 0, add_and_join(keep_ref[t], got_ref[t], model))


def join_kernel(mine_ref, theirs_ref, out_ref, *, model):
    put(out_ref, 0, add_and_join(mine_ref[...], theirs_ref[...], model))


def final_kernel(where_ref, *refs, model, seqs, chunks, parts):
    outs = refs[-5:]
    grad_ref, context_ref = outs[:2]
    ins = refs[: -5 - parts]
    moved = refs[-5 - parts : -5]
    if len(ins) == 2:
        total = ins[0][:, :model]
        mine = ins[0][:, model:]
        far = ins[1][...]
    else:
        total, mine, near = add_and_join(ins[0][...], ins[1][...], model)
        mine = jnp.concatenate([mine, near], axis=1)
        far = ins[2][...]
    grad_ref[...] = (total.astype(F32) + far[:, :model].astype(F32)).astype(BF16)
    theirs = far[:, model:]
    groups = seqs * chunks
    width = model // groups
    values = [mine[:, k * width : (k + 1) * width] for k in range(groups // 2)]
    values += [theirs[:, k * width : (k + 1) * width] for k in range(groups // 2)]
    own = where_ref[0] + where_ref[2] * chunks
    bit = 1
    while bit < groups:
        flip = (own & bit) != 0
        values = [jnp.where(flip, values[o ^ bit], values[o]) for o in range(groups)]
        bit *= 2
    for o in range(groups):
        lo = ((o % chunks) * seqs + o // chunks) * width
        context_ref[:, lo : lo + width] = values[o]
    for m in range(3):
        sums = []
        for i in range(seqs):
            acc = moved[i][:, m * width : (m + 1) * width].astype(F32)
            for j in range(i + seqs, parts, seqs):
                acc = acc + moved[j][:, m * width : (m + 1) * width].astype(F32)
            sums.append(acc)
        if seqs == 1:
            outs[2 + m][...] = sums[0]
        else:
            flip = where_ref[2] != 0
            outs[2 + m][:, :width] = jnp.where(flip, sums[1], sums[0])
            outs[2 + m][:, width:] = jnp.where(flip, sums[0], sums[1])


def pack_kernel(where_ref, blocks_ref, *refs, lefts, seqs, chunks, width, noted, halves):
    tokens, up = refs[:2]
    weight_refs = refs[2:5]
    hops = len(lefts)
    sends = refs[5 : 5 + hops]
    own_up = refs[5 + hops]
    weight_sends = refs[6 + hops : 6 + hops + seqs]
    half_sends = refs[6 + hops + seqs : 6 + hops + seqs + halves]
    note, blocks, sems = refs[6 + hops + seqs + halves :]
    fetch = pltpu.make_async_copy(blocks_ref, blocks, sems.at[sems.shape[0] - 1])
    fetch.start()
    model = tokens.shape[1]

    def columns(offset):
        which = (where_ref[0] ^ (offset % chunks)) * seqs + (where_ref[2] ^ (offset // chunks))
        return pl.ds(pl.multiple_of(which * width, width), width)

    copies = []
    for send, left in zip(sends, lefts):
        copies.append((tokens, send.at[:, :model]))
        for k in range(left):
            lo = model + k * width
            copies.append((up.at[:, columns(left + k)], send.at[:, lo : lo + width]))
    copies.append((up.at[:, columns(0)], own_up))
    for i in range(seqs):
        for m in range(3):
            source = weight_refs[m].at[:, columns(i * chunks)]
            lanes = slice(m * width, (m + 1) * width)
            copies.append((source, weight_sends[i].at[:, lanes]))
            if i < halves:
                size = half_sends[i].shape[0]
                part = pl.ds(pl.multiple_of(where_ref[3] * size, size), size)
                source = weight_refs[m].at[part, columns(i * chunks)]
                copies.append((source, half_sends[i].at[:, lanes]))
    copies = [
        pltpu.make_async_copy(source, target, sems.at[index])
        for index, (source, target) in enumerate(copies)
    ]
    for copy in copies:
        copy.start()
    fetch.wait()
    if noted:
        lane = lax.broadcasted_iota(jnp.int32, note.shape, 1)
        note[...] = jnp.where(lane < 64, blocks[0, 0], blocks[0, 1]).astype(F32).astype(BF16)
        lo = model + lefts[0] * width
        sends[0][:, lo : lo + 128] = note[...]
    for copy in copies:
        copy.wait()


def per_device(tokens, global_blocks, w_query, w_key, w_value, d_context):
    own_tokens = tokens[0]
    upstream = d_context[0]
    rows, model = own_tokens.shape
    hdim = model // HEADS
    chunks = lax.axis_size("ctx")
    parts = lax.axis_size("dp")
    seqs = 1
    if chunks == 4 and parts % 2 == 0 and model % 1024 == 0 and HEADS % 8 == 0 and rows % 32 == 0:
        seqs = 2
    groups = chunks * seqs
    width = model // groups
    heads = width // hdim
    position = lax.axis_index("ctx")
    line = lax.axis_index("dp")
    side = line % seqs

    where = jnp.stack([position, line, side, lax.axis_index("groups")]).astype(jnp.int32)
    hops = [("dp", 1, chunks)] if seqs == 2 else []
    bit = chunks // 2
    while bit:
        hops.append(("ctx", bit, bit))
        bit //= 2

    smem = pl.BlockSpec(memory_space=pltpu.SMEM)
    vmem = pl.BlockSpec(memory_space=pltpu.VMEM)
    hbm = pl.BlockSpec(memory_space=pltpu.HBM)
    chosen = global_blocks[0]
    lefts = [groups >> (k + 1) for k in range(len(hops))]
    packed = width % 128 == 0
    noted = 128 if seqs == 2 else 0
    halves = 1 if seqs == 2 and lax.axis_size("groups") == 2 else 0
    if packed:
        sizes = [model + left * width + (noted if k == 0 else 0) for k, left in enumerate(lefts)]
        outs = pl.pallas_call(
            lambda *refs: pack_kernel(
                *refs,
                lefts=lefts,
                seqs=seqs,
                chunks=chunks,
                width=width,
                noted=noted,
                halves=halves,
            ),
            out_shape=tuple(jax.ShapeDtypeStruct((rows, size), BF16) for size in sizes + [width])
            + (jax.ShapeDtypeStruct((model // parts, 3 * width), BF16),) * seqs
            + (jax.ShapeDtypeStruct((model // parts // 2, 3 * width), BF16),) * halves,
            in_specs=[smem] + [hbm] * 6,
            out_specs=(vmem,) * (len(hops) + 1 + seqs + halves),
            scratch_shapes=[
                pltpu.VMEM((rows, 128), BF16),
                pltpu.SMEM((1, 2), jnp.int32),
                pltpu.SemaphoreType.DMA((len(hops) + sum(lefts) + 2 + 3 * (seqs + halves),)),
            ],
            compiler_params=SMALL,
            cost_estimate=cost(2),
            name="pack",
        )(
            where,
            *[
                pltpu.with_memory_space_constraint(value, pltpu.HBM)
                for value in (global_blocks, own_tokens, upstream, w_query, w_key, w_value)
            ],
        )
        own_sends = outs[: len(hops)]
        own_up = outs[len(hops)]
        sends = outs[len(hops) + 1 : len(hops) + 1 + seqs]
        half_sends = outs[len(hops) + 1 + seqs :]
    else:

        def slice_of(value, offset):
            which = (position ^ (offset % chunks)) * seqs + (side ^ (offset // chunks))
            return lax.dynamic_slice_in_dim(value, which * width, width, 1)

        ups = [slice_of(upstream, o) for o in range(groups)]
        own_up = ups[0]
        own_sends = [
            jnp.concatenate([own_tokens] + ups[left : 2 * left], axis=1) for left in lefts
        ]
        sends = [
            jnp.concatenate(
                [slice_of(w, i * chunks) for w in (w_query, w_key, w_value)], axis=1
            )
            for i in range(seqs)
        ]

    arrived = [xor_permute(own_sends[k], *hops[k][:2]) for k in range(seqs)]
    weights = [sends[0]]
    shares = [(0, None)]
    fetched = []
    for j in range(1, parts):
        if j == 2 and halves:
            fetched.append(xor_permute(half_sends[j % seqs], "dp", j))
        else:
            weights.append(xor_permute(sends[j % seqs], "dp", j))
            shares.append((j, None))

    length = chunks * rows
    live = global_blocks[0, 0] >= 0

    def guarded(function, *operands):
        return lax.cond(
            live,
            function,
            lambda *values: jax.tree.map(
                lambda v: jnp.zeros(v.shape, v.dtype), jax.eval_shape(function, *values)
            ),
            *operands,
        )

    def attend(buffers, sources, weights, shares, carry=None, carried=(), far_ids=None):
        kind = F32 if carry == "out" else BF16
        results = pl.pallas_call(
            lambda *refs: attention_kernel(
                *refs,
                sources=sources,
                shares=shares,
                chunks=chunks,
                far_ids=far_ids,
                carry=carry,
                rows=rows,
                heads=heads,
                hdim=hdim,
                parts=parts,
                scale=1.0 / math.sqrt(hdim),
            ),
            out_shape=(jax.ShapeDtypeStruct((model // parts, 3 * width), kind),) * parts
            + (jax.ShapeDtypeStruct((chunks // 2, rows, model + width), BF16),) * 2,
            in_specs=[smem] * 2
            + [pl.BlockSpec(memory_space=pl.ANY)] * (len(buffers) + len(weights))
            + [vmem] * len(carried),
            out_specs=(vmem,) * (parts + 2),
            scratch_shapes=[
                pltpu.VMEM((length, model), BF16),
                pltpu.VMEM((model, 3 * width), BF16),
                pltpu.VMEM((length, width), BF16),
                pltpu.VMEM((heads, length, 2 * hdim), BF16),
                pltpu.VMEM((heads, 2 * hdim, length), BF16),
                pltpu.VMEM((heads, chunks, 2 * rows, 2 * hdim), BF16),
                pltpu.VMEM((heads, length, 2 * hdim), F32),
                pltpu.VMEM((length, 3 * width), BF16),
                pltpu.VMEM((length, width), BF16),
                pltpu.VMEM((16, 128), BF16),
                pltpu.SemaphoreType.DMA((2 * len(sources) + len(weights) + 1,)),
            ],
            compiler_params=pltpu.CompilerParams(vmem_limit_bytes=24 * 1024 * 1024),
            cost_estimate=cost(14 // seqs),
            name="attention",
        )(where, chosen, *buffers, *weights, *carried)
        return results[:parts], results[parts], results[parts + 1]

    def combine(keep, got):
        kinds = (jax.ShapeDtypeStruct((rows, model + 2 * width), BF16),) * keep.shape[0]
        return pl.pallas_call(
            lambda *refs: combine_kernel(*refs, model=model),
            out_shape=kinds,
            in_specs=[vmem] * 2,
            out_specs=(vmem,) * len(kinds),
            compiler_params=SMALL,
            cost_estimate=cost(1),
            name="combine",
        )(keep, got)

    def join(mine, theirs):
        return pl.pallas_call(
            lambda *refs: join_kernel(*refs, model=model),
            out_shape=jax.ShapeDtypeStruct((mine.shape[0], 2 * mine.shape[1] - model), BF16),
            in_specs=[vmem] * 2,
            out_specs=vmem,
            compiler_params=SMALL,
            cost_estimate=cost(1),
            name="join",
        )(mine, theirs)

    if seqs == 2:
        line_hop, far_hop, near_hop = [hop[:2] for hop in hops]
        tz, tx = arrived

        def share(own, tx, *fetched):
            rest = jnp.concatenate([tx[:, :model], tx[:, model + width :]], axis=1)
            shared = xor_permute(jnp.concatenate([own, rest], axis=0), *near_hop)
            return (shared, *[xor_permute(value, "groups", 1) for value in fetched])

        shared, *others = guarded(share, own_sends[2], tx, *fetched)
        tz, shared = lax.optimization_barrier((tz, shared))
        for j, (here, there) in enumerate(zip(fetched, others), 2):
            weights += [here, there]
            shares += [(j, 0), (j, 1)]

        def both(tz, tx, shared, own_tokens, own_up, *weights):
            lo = model + 2 * width
            part = rows // 2
            txz = [
                xor_permute(
                    jnp.concatenate([piece[:, :model], piece[:, lo : lo + 2 * width]], axis=1),
                    *far_hop,
                )
                for piece in (tz[:part], tz[part:])
            ]
            first, keep, send = attend(
                (own_tokens, shared, tx, own_up),
                (
                    (0, 0, rows, 3, 0),
                    (1, 0, rows, 1, model),
                    (2, 0, rows, 2, model),
                    (1, rows, rows, 1, model),
                ),
                weights,
                shares,
                carry="out",
            )
            first = list(first)
            txz, first[0] = lax.optimization_barrier((txz, first[0]))
            ctz = xor_permute(tz, *near_hop)
            ctxz = [xor_permute(piece, *near_hop) for piece in txz]
            up = model + width
            grad_w, keep_other, send_other = attend(
                (tz, ctz, *txz, *ctxz),
                (
                    (0, 0, rows, 0, model),
                    (1, 0, rows, 1, up),
                    (2, 0, part, 2, model),
                    (3, 0, part, 3, model),
                    (4, 0, part, 4, up),
                    (5, 0, part, 5, up),
                ),
                weights,
                shares,
                carry="in",
                carried=first,
                far_ids=model + 4 * width,
            )
            return grad_w, keep, send, keep_other, send_other

        grad_w, *rest = both(tz, tx, shared, own_tokens, own_up, *weights)

        keep, send, keep_other, send_other = rest
        got_other = xor_permute(send_other, *near_hop)
        got = xor_permute(send, *near_hop)
        moved = [grad_w[0]] + [xor_permute(grad_w[j], "dp", j) for j in range(1, parts)]

        def collect(keep, got, keep_other, got_other):
            held, far = combine(keep_other, got_other)
            far = xor_permute(join(held, xor_permute(far, *far_hop)), *line_hop)
            mine, near = combine(keep, got)
            return mine, xor_permute(near, *far_hop), far

        ins = guarded(collect, keep, got, keep_other, got_other)
    else:

        def spread(first, *own):
            pieces = {hops[0][2]: first}
            for k in range(1, len(hops)):
                axis, bit, offset = hops[k]
                lo = model + lefts[k] * width
                for key in list(pieces):
                    value = pieces[key]
                    value = jnp.concatenate(
                        [value[:, :model], value[:, lo : lo + lefts[k] * width]], axis=1
                    )
                    pieces[key + offset] = xor_permute(value, axis, bit)
                pieces[offset] = xor_permute(own[k - 1], axis, bit)
            return tuple(pieces[o] for o in range(1, groups))

        pieces = guarded(spread, arrived[0], *own_sends[1:])
        ups = [own_up] + [value[:, model : model + width] for value in pieces]
        buffers = [own_tokens] + [value[:, :model] for value in pieces] + ups
        grad_w, keep, send = attend(
            buffers, [(o, 0, rows, groups + o, 0) for o in range(groups)], weights, shares
        )

        def collect(keep, send):
            held = combine(keep, xor_permute(send, *hops[-1][:2]))
            for axis, bit, _ in reversed(hops[1:-1]):
                theirs = [xor_permute(value, axis, bit) for value in held[1::2]]
                held = [join(*pair) for pair in zip(held[::2], theirs)]
            return held[0], xor_permute(held[1], *hops[0][:2])

        moved = [grad_w[0]] + [xor_permute(grad_w[j], "dp", j) for j in range(1, parts)]
        ins = guarded(collect, keep, send)

    grad_tokens, context, *final = pl.pallas_call(
        lambda *refs: final_kernel(*refs, model=model, seqs=seqs, chunks=chunks, parts=parts),
        out_shape=(jax.ShapeDtypeStruct((rows, model), BF16),) * 2
        + (jax.ShapeDtypeStruct((model // parts, seqs * width), F32),) * 3,
        in_specs=[smem] + [vmem] * (len(ins) + len(moved)),
        compiler_params=SMALL,
        cost_estimate=cost(2),
        name="finish",
    )(where, *ins, *moved)
    return (context[None], grad_tokens[None], *final)


def solution(mesh):
    return jax.shard_map(
        per_device,
        mesh=mesh,
        in_specs=(
            P(("groups", "dp"), "ctx", None),
            P(("groups", "dp"), None),
            P("dp", None),
            P("dp", None),
            P("dp", None),
            P(("groups", "dp"), "ctx", None),
        ),
        out_specs=(
            P(("groups", "dp"), "ctx", None),
            P(("groups", "dp"), "ctx", None),
            P(("groups", "dp"), "ctx"),
            P(("groups", "dp"), "ctx"),
            P(("groups", "dp"), "ctx"),
        ),
        check_vma=False,
    )
```

```python
import math

import jax
import jax.numpy as jnp
from jax import lax
from jax.experimental import pallas as pl
from jax.experimental.pallas import tpu as pltpu
from jax.sharding import PartitionSpec as P

HEADS = 16
BLK = 64
NEG = -1e30
SPAN = 4

NT = (((1,), (1,)), ((), ()))
TN = (((0,), (0,)), ((), ()))
F32 = jnp.float32
BF16 = jnp.bfloat16


SMALL = pltpu.CompilerParams(vmem_limit_bytes=8 * 1024 * 1024)


def cost(micros):
    return pl.CostEstimate(
        flops=0, transcendentals=0, bytes_accessed=int(micros * 3_000_000)
    )


def xor_permute(value, axis, bit):
    count = lax.axis_size(axis)
    return lax.ppermute(value, axis, [(i, i ^ bit) for i in range(count)])


def attention_kernel(
    where_ref, chosen_ref, *refs, sources, shares, chunks, far_ids, carry, rows, heads, hdim, parts, scale
):
    half = chunks // 2
    count = 1 + max(max(source[0], source[3]) for source in sources)
    buffers = refs[:count]
    weight_refs = refs[count : count + len(shares)]
    refs = refs[count + len(shares) :]
    carried = refs[:parts] if carry == "in" else None
    outs = refs[parts:] if carry == "in" else refs
    grad_w_refs = outs[:parts]
    keep_ref, send_ref = outs[parts : parts + 2]
    (
        all_tokens, weight, up_all, kv_s, kvt_s, pair_s, dkv_s, grads, context_s, noted, sems
    ) = outs[parts + 2 :]
    length = chunks * rows
    width = heads * hdim
    model = all_tokens.shape[1]
    part_rows = model // parts
    position = where_ref[0]
    line = where_ref[1]

    copies = []
    for ref, (j, side) in zip(weight_refs, shares):
        size = ref.shape[0]
        start = (line ^ j) * part_rows
        if side is not None:
            start = start + (where_ref[3] ^ side) * size
        target = pl.ds(pl.multiple_of(start, size), size)
        copies.append((ref, weight.at[target, :]))
    at = 0
    for index, first, size, up, start in sources:
        target = pl.ds(at, size)
        held = pl.ds(first, size)
        copies.append((buffers[index].at[held, :model], all_tokens.at[target, :]))
        if up != index:
            held = pl.ds(0, size)
        copies.append((buffers[up].at[held, start : start + width], up_all.at[target, :]))
        at += size
    if far_ids is not None:
        copies.append((buffers[0].at[:16, far_ids : far_ids + 128], noted))
    copies = [
        pltpu.make_async_copy(source, target, sems.at[index])
        for index, (source, target) in enumerate(copies)
    ]
    for copy in copies:
        copy.start()
    pair_s[...] = jnp.zeros_like(pair_s)
    if SPAN < chunks:
        dkv_s[...] = jnp.zeros_like(dkv_s)
    for copy in copies:
        copy.wait()
    if far_ids is None:
        chosen = [chosen_ref[k] for k in range(2)]
    else:
        chosen = [noted[:1, 64 * k : 64 * k + 1].astype(F32).astype(jnp.int32) for k in range(2)]
        chosen = [jnp.broadcast_to(value, (1, rows)) for value in chosen]

    tile = min(512, length)

    @pl.loop(0, length // tile, unroll=length == tile)
    def _(t):
        at = pl.ds(pl.multiple_of(t * tile, tile), tile)
        out = jnp.dot(all_tokens[at, :], weight[...], preferred_element_type=F32)
        for h in range(heads):
            lo = h * hdim
            kv = jnp.concatenate(
                [
                    out[:, width + lo : width + lo + hdim],
                    out[:, 2 * width + lo : 2 * width + lo + hdim],
                ],
                axis=1,
            )
            kv_s[h, at, :] = kv.astype(BF16)
            kvt_s[h, :, at] = jnp.transpose(kv).astype(BF16)
            q = (out[:, lo : lo + hdim].astype(BF16) * scale).astype(BF16)
            for p in range(tile // rows):
                pair_s[h, t * (tile // rows) + p, :rows, :hdim] = q[p * rows : (p + 1) * rows]
    for h in range(heads):
        for b in range(chunks):
            pair_s[h, b, rows:, hdim:] = up_all[
                b * rows : (b + 1) * rows, h * hdim : (h + 1) * hdim
            ]

    blocks_per_chunk = rows // BLK
    block_count = length // BLK
    log_blocks = int(math.log2(blocks_per_chunk))

    span = min(SPAN, chunks)

    @pl.loop(0, chunks // span, unroll=chunks == span)
    def _(t):
        first, second = chosen
        shape = (block_count, 1, rows)
        key = lax.broadcasted_iota(jnp.int32, shape, 0)
        key_block = (lax.shift_right_logical(key, log_blocks) ^ position) * blocks_per_chunk + (
            key & (blocks_per_chunk - 1)
        )
        offset = lax.shift_right_logical(
            lax.broadcasted_iota(jnp.int32, shape, 2), int(math.log2(BLK))
        )
        biases = []
        for p in range(span):
            j = t * span + p
            query_block = (position ^ j) * blocks_per_chunk + offset
            keep = (
                (jnp.abs(key_block - query_block) <= 1)
                | (key_block == first)
                | (key_block == second)
                | (query_block == first)
                | (query_block == second)
            )
            biases.append(jnp.where(keep, 0.0, NEG))
        for h in range(heads):
            pair = pair_s[h, pl.ds(t * span, span)].reshape(span * 2 * rows, 2 * hdim)
            both = lax.dot_general(kv_s[h], pair, NT, preferred_element_type=F32)
            parts_of = [both[:, p * rows : (p + 1) * rows] for p in range(2 * span)]
            forward = []
            backward = []
            inverses = []
            for p in range(span):
                scores = parts_of[2 * p].reshape(block_count, BLK, rows) + biases[p]
                scores = scores.reshape(length, rows)
                grad_probs = parts_of[2 * p + 1]
                raw = jnp.exp(scores - jnp.max(scores, axis=0, keepdims=True))
                inverse = 1.0 / jnp.sum(raw, axis=0, keepdims=True)
                raw_low = raw.astype(BF16)
                probs = raw * inverse
                delta = inverse * jnp.sum(
                    raw_low.astype(F32) * grad_probs, axis=0, keepdims=True
                )
                low = (probs * (grad_probs - delta)).astype(BF16)
                forward += [raw_low, low]
                backward += [low, probs.astype(BF16)]
                inverses.append(inverse)
            sums = jnp.dot(
                kvt_s[h],
                jnp.concatenate(forward, axis=1),
                preferred_element_type=F32,
            )
            dkv = jnp.dot(
                jnp.concatenate(backward, axis=1), pair, preferred_element_type=F32
            )
            if span == chunks:
                dkv_s[h] = dkv
            else:
                dkv_s[h] += dkv
            lo = h * hdim
            for p in range(span):
                at = pl.ds(pl.multiple_of((t * span + p) * rows, rows), rows)
                lanes = 2 * p * rows
                rows_out = jnp.transpose(
                    jnp.concatenate(
                        [
                            sums[:hdim, lanes + rows : lanes + 2 * rows] * scale,
                            sums[hdim:, lanes : lanes + rows] * inverses[p],
                        ],
                        axis=0,
                    )
                ).astype(BF16)
                grads[at, lo : lo + hdim] = rows_out[:, :hdim]
                context_s[at, lo : lo + hdim] = rows_out[:, hdim:]

    for h in range(heads):
        lo = h * hdim
        grads[:, width + lo : width + lo + hdim] = dkv_s[h, :, :hdim].astype(BF16)
        grads[:, 2 * width + lo : 2 * width + lo + hdim] = dkv_s[h, :, hdim:].astype(BF16)

    for j in range(parts):
        cols = pl.ds(pl.multiple_of((line ^ j) * part_rows, part_rows), part_rows)
        out = lax.dot_general(all_tokens[:, cols], grads[...], TN, preferred_element_type=F32)
        if carry == "in":
            out = out + carried[j][...]
        grad_w_refs[j][...] = out.astype(grad_w_refs[j].dtype)

    @pl.loop(0, half, unroll=half == 2)
    def _(t):
        at = pl.ds(pl.multiple_of(t * 2 * rows, 2 * rows), 2 * rows)
        out = lax.dot_general(grads[at, :], weight[...], NT, preferred_element_type=F32)
        keep_ref[t, :, :model] = out[:rows].astype(BF16)
        send_ref[t, :, :model] = out[rows:].astype(BF16)
        keep_ref[t, :, model:] = context_s[pl.ds(pl.multiple_of(t * 2 * rows, rows), rows), :]
        send_ref[t, :, model:] = context_s[
            pl.ds(pl.multiple_of(t * 2 * rows + rows, rows), rows), :
        ]


def add_and_join(mine, theirs, model):
    total = (mine[:, :model].astype(F32) + theirs[:, :model].astype(F32)).astype(BF16)
    return [total, mine[:, model:], theirs[:, model:]]


def put(out_ref, first, values):
    size = values[0].shape[0]
    lo = 0
    for value in values:
        out_ref[first : first + size, lo : lo + value.shape[1]] = value
        lo += value.shape[1]


def combine_kernel(keep_ref, got_ref, *outs, model):
    for t in range(keep_ref.shape[0]):
        put(outs[t], 0, add_and_join(keep_ref[t], got_ref[t], model))


def join_kernel(mine_ref, theirs_ref, out_ref, *, model):
    put(out_ref, 0, add_and_join(mine_ref[...], theirs_ref[...], model))


def final_kernel(where_ref, *refs, model, seqs, chunks, parts):
    outs = refs[-5:]
    grad_ref, context_ref = outs[:2]
    ins = refs[: -5 - parts]
    moved = refs[-5 - parts : -5]
    if len(ins) == 2:
        total = ins[0][:, :model]
        mine = ins[0][:, model:]
        far = ins[1][...]
    else:
        total, mine, near = add_and_join(ins[0][...], ins[1][...], model)
        mine = jnp.concatenate([mine, near], axis=1)
        far = ins[2][...]
    grad_ref[...] = (total.astype(F32) + far[:, :model].astype(F32)).astype(BF16)
    theirs = far[:, model:]
    groups = seqs * chunks
    width = model // groups
    values = [mine[:, k * width : (k + 1) * width] for k in range(groups // 2)]
    values += [theirs[:, k * width : (k + 1) * width] for k in range(groups // 2)]
    own = where_ref[0] + where_ref[2] * chunks
    bit = 1
    while bit < groups:
        flip = (own & bit) != 0
        values = [jnp.where(flip, values[o ^ bit], values[o]) for o in range(groups)]
        bit *= 2
    for o in range(groups):
        lo = ((o % chunks) * seqs + o // chunks) * width
        context_ref[:, lo : lo + width] = values[o]
    for m in range(3):
        sums = []
        for i in range(seqs):
            acc = moved[i][:, m * width : (m + 1) * width].astype(F32)
            for j in range(i + seqs, parts, seqs):
                acc = acc + moved[j][:, m * width : (m + 1) * width].astype(F32)
            sums.append(acc)
        if seqs == 1:
            outs[2 + m][...] = sums[0]
        else:
            flip = where_ref[2] != 0
            outs[2 + m][:, :width] = jnp.where(flip, sums[1], sums[0])
            outs[2 + m][:, width:] = jnp.where(flip, sums[0], sums[1])


def pack_kernel(where_ref, blocks_ref, *refs, lefts, seqs, chunks, width, noted, halves):
    tokens, up = refs[:2]
    weight_refs = refs[2:5]
    hops = len(lefts)
    sends = refs[5 : 5 + hops]
    own_up = refs[5 + hops]
    weight_sends = refs[6 + hops : 6 + hops + seqs]
    half_sends = refs[6 + hops + seqs : 6 + hops + seqs + halves]
    note, blocks, sems = refs[6 + hops + seqs + halves :]
    fetch = pltpu.make_async_copy(blocks_ref, blocks, sems.at[sems.shape[0] - 1])
    fetch.start()
    model = tokens.shape[1]

    def columns(offset):
        which = (where_ref[0] ^ (offset % chunks)) * seqs + (where_ref[2] ^ (offset // chunks))
        return pl.ds(pl.multiple_of(which * width, width), width)

    copies = []
    for send, left in zip(sends, lefts):
        copies.append((tokens, send.at[:, :model]))
        for k in range(left):
            lo = model + k * width
            copies.append((up.at[:, columns(left + k)], send.at[:, lo : lo + width]))
    copies.append((up.at[:, columns(0)], own_up))
    for i in range(seqs):
        for m in range(3):
            source = weight_refs[m].at[:, columns(i * chunks)]
            lanes = slice(m * width, (m + 1) * width)
            copies.append((source, weight_sends[i].at[:, lanes]))
            if i < halves:
                size = half_sends[i].shape[0]
                part = pl.ds(pl.multiple_of(where_ref[3] * size, size), size)
                source = weight_refs[m].at[part, columns(i * chunks)]
                copies.append((source, half_sends[i].at[:, lanes]))
    copies = [
        pltpu.make_async_copy(source, target, sems.at[index])
        for index, (source, target) in enumerate(copies)
    ]
    for copy in copies:
        copy.start()
    fetch.wait()
    if noted:
        lane = lax.broadcasted_iota(jnp.int32, note.shape, 1)
        note[...] = jnp.where(lane < 64, blocks[0, 0], blocks[0, 1]).astype(F32).astype(BF16)
        lo = model + lefts[0] * width
        sends[0][:, lo : lo + 128] = note[...]
    for copy in copies:
        copy.wait()


def per_device(tokens, global_blocks, w_query, w_key, w_value, d_context):
    own_tokens = tokens[0]
    upstream = d_context[0]
    rows, model = own_tokens.shape
    hdim = model // HEADS
    chunks = lax.axis_size("ctx")
    parts = lax.axis_size("dp")
    seqs = 1
    if chunks == 4 and parts % 2 == 0 and model % 1024 == 0 and HEADS % 8 == 0 and rows % 32 == 0:
        seqs = 2
    groups = chunks * seqs
    width = model // groups
    heads = width // hdim
    position = lax.axis_index("ctx")
    line = lax.axis_index("dp")
    side = line % seqs

    where = jnp.stack([position, line, side, lax.axis_index("groups")]).astype(jnp.int32)
    hops = [("dp", 1, chunks)] if seqs == 2 else []
    bit = chunks // 2
    while bit:
        hops.append(("ctx", bit, bit))
        bit //= 2

    smem = pl.BlockSpec(memory_space=pltpu.SMEM)
    vmem = pl.BlockSpec(memory_space=pltpu.VMEM)
    hbm = pl.BlockSpec(memory_space=pltpu.HBM)
    chosen = global_blocks[0]
    lefts = [groups >> (k + 1) for k in range(len(hops))]
    packed = width % 128 == 0
    noted = 128 if seqs == 2 else 0
    halves = 1 if seqs == 2 and lax.axis_size("groups") == 2 else 0
    if packed:
        sizes = [model + left * width + (noted if k == 0 else 0) for k, left in enumerate(lefts)]
        outs = pl.pallas_call(
            lambda *refs: pack_kernel(
                *refs,
                lefts=lefts,
                seqs=seqs,
                chunks=chunks,
                width=width,
                noted=noted,
                halves=halves,
            ),
            out_shape=tuple(jax.ShapeDtypeStruct((rows, size), BF16) for size in sizes + [width])
            + (jax.ShapeDtypeStruct((model // parts, 3 * width), BF16),) * seqs
            + (jax.ShapeDtypeStruct((model // parts // 2, 3 * width), BF16),) * halves,
            in_specs=[smem] + [hbm] * 6,
            out_specs=(vmem,) * (len(hops) + 1 + seqs + halves),
            scratch_shapes=[
                pltpu.VMEM((rows, 128), BF16),
                pltpu.SMEM((1, 2), jnp.int32),
                pltpu.SemaphoreType.DMA((len(hops) + sum(lefts) + 2 + 3 * (seqs + halves),)),
            ],
            compiler_params=SMALL,
            cost_estimate=cost(2),
            name="pack",
        )(
            where,
            *[
                pltpu.with_memory_space_constraint(value, pltpu.HBM)
                for value in (global_blocks, own_tokens, upstream, w_query, w_key, w_value)
            ],
        )
        own_sends = outs[: len(hops)]
        own_up = outs[len(hops)]
        sends = outs[len(hops) + 1 : len(hops) + 1 + seqs]
        half_sends = outs[len(hops) + 1 + seqs :]
    else:

        def slice_of(value, offset):
            which = (position ^ (offset % chunks)) * seqs + (side ^ (offset // chunks))
            return lax.dynamic_slice_in_dim(value, which * width, width, 1)

        ups = [slice_of(upstream, o) for o in range(groups)]
        own_up = ups[0]
        own_sends = [
            jnp.concatenate([own_tokens] + ups[left : 2 * left], axis=1) for left in lefts
        ]
        sends = [
            jnp.concatenate(
                [slice_of(w, i * chunks) for w in (w_query, w_key, w_value)], axis=1
            )
            for i in range(seqs)
        ]

    arrived = [xor_permute(own_sends[k], *hops[k][:2]) for k in range(seqs)]
    weights = [sends[0]]
    shares = [(0, None)]
    fetched = []
    for j in range(1, parts):
        if j == 2 and halves:
            fetched.append(xor_permute(half_sends[j % seqs], "dp", j))
        else:
            weights.append(xor_permute(sends[j % seqs], "dp", j))
            shares.append((j, None))

    length = chunks * rows
    live = global_blocks[0, 0] >= 0

    def guarded(function, *operands):
        return lax.cond(
            live,
            function,
            lambda *values: jax.tree.map(
                lambda v: jnp.zeros(v.shape, v.dtype), jax.eval_shape(function, *values)
            ),
            *operands,
        )

    def attend(buffers, sources, weights, shares, carry=None, carried=(), far_ids=None):
        kind = F32 if carry == "out" else BF16
        results = pl.pallas_call(
            lambda *refs: attention_kernel(
                *refs,
                sources=sources,
                shares=shares,
                chunks=chunks,
                far_ids=far_ids,
                carry=carry,
                rows=rows,
                heads=heads,
                hdim=hdim,
                parts=parts,
                scale=1.0 / math.sqrt(hdim),
            ),
            out_shape=(jax.ShapeDtypeStruct((model // parts, 3 * width), kind),) * parts
            + (jax.ShapeDtypeStruct((chunks // 2, rows, model + width), BF16),) * 2,
            in_specs=[smem] * 2
            + [pl.BlockSpec(memory_space=pl.ANY)] * (len(buffers) + len(weights))
            + [vmem] * len(carried),
            out_specs=(vmem,) * (parts + 2),
            scratch_shapes=[
                pltpu.VMEM((length, model), BF16),
                pltpu.VMEM((model, 3 * width), BF16),
                pltpu.VMEM((length, width), BF16),
                pltpu.VMEM((heads, length, 2 * hdim), BF16),
                pltpu.VMEM((heads, 2 * hdim, length), BF16),
                pltpu.VMEM((heads, chunks, 2 * rows, 2 * hdim), BF16),
                pltpu.VMEM((heads, length, 2 * hdim), F32),
                pltpu.VMEM((length, 3 * width), BF16),
                pltpu.VMEM((length, width), BF16),
                pltpu.VMEM((16, 128), BF16),
                pltpu.SemaphoreType.DMA((2 * len(sources) + len(weights) + 1,)),
            ],
            compiler_params=pltpu.CompilerParams(vmem_limit_bytes=24 * 1024 * 1024),
            cost_estimate=cost(14 // seqs),
            name="attention",
        )(where, chosen, *buffers, *weights, *carried)
        return results[:parts], results[parts], results[parts + 1]

    def combine(keep, got):
        kinds = (jax.ShapeDtypeStruct((rows, model + 2 * width), BF16),) * keep.shape[0]
        return pl.pallas_call(
            lambda *refs: combine_kernel(*refs, model=model),
            out_shape=kinds,
            in_specs=[vmem] * 2,
            out_specs=(vmem,) * len(kinds),
            compiler_params=SMALL,
            cost_estimate=cost(1),
            name="combine",
        )(keep, got)

    def join(mine, theirs):
        return pl.pallas_call(
            lambda *refs: join_kernel(*refs, model=model),
            out_shape=jax.ShapeDtypeStruct((mine.shape[0], 2 * mine.shape[1] - model), BF16),
            in_specs=[vmem] * 2,
            out_specs=vmem,
            compiler_params=SMALL,
            cost_estimate=cost(1),
            name="join",
        )(mine, theirs)

    if seqs == 2:
        line_hop, far_hop, near_hop = [hop[:2] for hop in hops]
        tz, tx = arrived

        def share(own, tx, *fetched):
            rest = jnp.concatenate([tx[:, :model], tx[:, model + width :]], axis=1)
            shared = xor_permute(jnp.concatenate([own, rest], axis=0), *near_hop)
            return (shared, *[xor_permute(value, "groups", 1) for value in fetched])

        shared, *others = guarded(share, own_sends[2], tx, *fetched)
        tz, shared = lax.optimization_barrier((tz, shared))
        for j, (here, there) in enumerate(zip(fetched, others), 2):
            weights += [here, there]
            shares += [(j, 0), (j, 1)]

        def both(tz, tx, shared, own_tokens, own_up, *weights):
            lo = model + 2 * width
            part = rows // 2
            txz = [
                xor_permute(
                    jnp.concatenate([piece[:, :model], piece[:, lo : lo + 2 * width]], axis=1),
                    *far_hop,
                )
                for piece in (tz[:part], tz[part:])
            ]
            first, keep, send = attend(
                (own_tokens, shared, tx, own_up),
                (
                    (0, 0, rows, 3, 0),
                    (1, 0, rows, 1, model),
                    (2, 0, rows, 2, model),
                    (1, rows, rows, 1, model),
                ),
                weights,
                shares,
                carry="out",
            )
            first = list(first)
            txz, first[0] = lax.optimization_barrier((txz, first[0]))
            ctz = xor_permute(tz, *near_hop)
            ctxz = [xor_permute(piece, *near_hop) for piece in txz]
            up = model + width
            grad_w, keep_other, send_other = attend(
                (tz, ctz, *txz, *ctxz),
                (
                    (0, 0, rows, 0, model),
                    (1, 0, rows, 1, up),
                    (2, 0, part, 2, model),
                    (3, 0, part, 3, model),
                    (4, 0, part, 4, up),
                    (5, 0, part, 5, up),
                ),
                weights,
                shares,
                carry="in",
                carried=first,
                far_ids=model + 4 * width,
            )
            return grad_w, keep, send, keep_other, send_other

        grad_w, *rest = both(tz, tx, shared, own_tokens, own_up, *weights)

        keep, send, keep_other, send_other = rest
        got_other = xor_permute(send_other, *near_hop)
        got = xor_permute(send, *near_hop)
        moved = [grad_w[0]] + [xor_permute(grad_w[j], "dp", j) for j in range(1, parts)]

        def collect(keep, got, keep_other, got_other):
            held, far = combine(keep_other, got_other)
            far = xor_permute(join(held, xor_permute(far, *far_hop)), *line_hop)
            mine, near = combine(keep, got)
            return mine, xor_permute(near, *far_hop), far

        ins = guarded(collect, keep, got, keep_other, got_other)
    else:

        def spread(first, *own):
            pieces = {hops[0][2]: first}
            for k in range(1, len(hops)):
                axis, bit, offset = hops[k]
                lo = model + lefts[k] * width
                for key in list(pieces):
                    value = pieces[key]
                    value = jnp.concatenate(
                        [value[:, :model], value[:, lo : lo + lefts[k] * width]], axis=1
                    )
                    pieces[key + offset] = xor_permute(value, axis, bit)
                pieces[offset] = xor_permute(own[k - 1], axis, bit)
            return tuple(pieces[o] for o in range(1, groups))

        pieces = guarded(spread, arrived[0], *own_sends[1:])
        ups = [own_up] + [value[:, model : model + width] for value in pieces]
        buffers = [own_tokens] + [value[:, :model] for value in pieces] + ups
        grad_w, keep, send = attend(
            buffers, [(o, 0, rows, groups + o, 0) for o in range(groups)], weights, shares
        )

        def collect(keep, send):
            held = combine(keep, xor_permute(send, *hops[-1][:2]))
            for axis, bit, _ in reversed(hops[1:-1]):
                theirs = [xor_permute(value, axis, bit) for value in held[1::2]]
                held = [join(*pair) for pair in zip(held[::2], theirs)]
            return held[0], xor_permute(held[1], *hops[0][:2])

        moved = [grad_w[0]] + [xor_permute(grad_w[j], "dp", j) for j in range(1, parts)]
        ins = guarded(collect, keep, send)

    grad_tokens, context, *final = pl.pallas_call(
        lambda *refs: final_kernel(*refs, model=model, seqs=seqs, chunks=chunks, parts=parts),
        out_shape=(jax.ShapeDtypeStruct((rows, model), BF16),) * 2
        + (jax.ShapeDtypeStruct((model // parts, seqs * width), F32),) * 3,
        in_specs=[smem] + [vmem] * (len(ins) + len(moved)),
        compiler_params=SMALL,
        cost_estimate=cost(2),
        name="finish",
    )(where, *ins, *moved)
    return (context[None], grad_tokens[None], *final)


def solution(mesh):
    return jax.shard_map(
        per_device,
        mesh=mesh,
        in_specs=(
            P(("groups", "dp"), "ctx", None),
            P(("groups", "dp"), None),
            P("dp", None),
            P("dp", None),
            P("dp", None),
            P(("groups", "dp"), "ctx", None),
        ),
        out_specs=(
            P(("groups", "dp"), "ctx", None),
            P(("groups", "dp"), "ctx", None),
            P(("groups", "dp"), "ctx"),
            P(("groups", "dp"), "ctx"),
            P(("groups", "dp"), "ctx"),
        ),
        check_vma=False,
    )
```
